256 devices in a mesh: sub: 16 (over z, core), dom: 16 (over y, x).
Axes of the slice: x: 4, y: 4, z: 8, core: 2. Of those that a mesh axis runs over, the one named last changes fastest.
Arguments:
- start_vectors: float32 [16, 3, 64, 16, 16, 128], P('sub', None, None, 'dom'), may hold values from -6 to 6
- face_x: float32 [16, 16, 16, 128], P('sub', 'dom'), may hold values from 0.1 to 10
- face_y: float32 [16, 16, 16, 128], P('sub', 'dom'), may hold values from 0.1 to 10
- face_z: float32 [16, 16, 16, 128], P('sub', 'dom'), may hold values from 0.1 to 10
- masses: float32 [16, 16, 16, 128], P('sub', 'dom'), may hold values from 0.5 to 2
- active: int32 [16], P('sub'), may hold values from 8 to 16, as said below
Outputs:
- deflation: bfloat16 [16, 3, 64, 16, 16, 128], P('sub', None, None, 'dom')
- coarse_diag: float32 [16, 64, 64], P('sub')
- coarse_off: float32 [16, 64, 64], P('sub')
The draws below stay inside these ranges and needn't reach their ends.
Inputs may be any that keep to these rules, and one draw needn't show every extreme that they name: `active`: some subdomain has all 16 planes.
All inputs are finite; a program needn't handle non-finite values.
Results may differ from the reference program's by a relative error of at most 0.001.
Values sent between devices are 32-bit elements; how exact they have to be, the bound alone decides.
No kernel may reach another device: no remote copies, remote signals or barrier semaphores. Data moves between devices by JAX's collectives and lax.ppermute only.
A program may use at most 64 MiB of HBM per device.

```python
import math
import jax
import jax.numpy as jnp
from jax import lax

K = 64
NXS = 16
NZ = 128
OV = 4
STEPS = 2
SUBS = 16
NY = 16


def draw_active(key, part):
    base = jax.random.fold_in(key, 7)
    first_key, second_key = jax.random.split(base)
    counts = jax.random.randint(first_key, (SUBS,), NXS // 2, NXS + 1, dtype=jnp.int32)
    chosen = jax.random.randint(second_key, (), 0, SUBS, dtype=jnp.int32)
    return jnp.where(jnp.arange(SUBS, dtype=jnp.int32) == chosen, NXS, counts).astype(jnp.int32)


def steps_of(rng, dims, cuts, least, high):
    gain, own = 1.0, jax.random.fold_in(rng, 6)
    for dim, parts in cuts:
        draws = jnp.exp(jax.random.uniform(jax.random.fold_in(own, dim), (parts,), jnp.float32, least / len(cuts), high / len(cuts)))
        gain = gain * jnp.repeat(draws, dims[dim] // parts).reshape([-1 if axis == dim else 1 for axis in range(len(dims))])
    return gain


def bell_draw(key, shape, width, reach, cuts=(), held_as=jnp.bfloat16):
    gain = steps_of(key, shape, cuts, -0.22, 0.18) if cuts else 1.0
    drawn = jax.random.normal(key, shape, jnp.float32) * width * gain
    return jnp.minimum(jnp.maximum(drawn, -reach), reach).astype(held_as)


def setup_inputs(seed: int = 0) -> dict:
    arg_keys = jax.random.split(jax.random.key(seed), 7)
    return {
        "start_vectors": bell_draw(arg_keys[0], (SUBS, 3, K, NY, NXS, NZ), 1.0, 6.0, ((0, 16), (3, 16)), jnp.float32),
        "face_x": jnp.clip(jnp.exp(math.log(10.0) - 4.6051702 * jax.random.uniform(arg_keys[1], (SUBS, NY, NXS, NZ), jnp.float32) ** steps_of(arg_keys[1], (SUBS, NY, NXS, NZ), ((0, 16), (1, 16)), -0.2, 0.2)), 0.1, 10.0),
        "face_y": jnp.clip(jnp.exp(math.log(10.0) - 4.6051702 * jax.random.uniform(arg_keys[2], (SUBS, NY, NXS, NZ), jnp.float32) ** steps_of(arg_keys[2], (SUBS, NY, NXS, NZ), ((0, 16), (1, 16)), -0.2, 0.2)), 0.1, 10.0),
        "face_z": jnp.clip(jnp.exp(math.log(10.0) - 4.6051702 * jax.random.uniform(arg_keys[3], (SUBS, NY, NXS, NZ), jnp.float32) ** steps_of(arg_keys[3], (SUBS, NY, NXS, NZ), ((0, 16), (1, 16)), -0.2, 0.2)), 0.1, 10.0),
        "masses": jnp.clip(jnp.exp(math.log(2.0) - 1.3862944 * jax.random.uniform(arg_keys[4], (SUBS, NY, NXS, NZ), jnp.float32) ** steps_of(arg_keys[4], (SUBS, NY, NXS, NZ), ((0, 16), (1, 16)), -0.2, 0.2)), 0.5, 2.0),
        "active": draw_active(jax.random.fold_in(arg_keys[6], 71), 0),
    }


def gram_of(left, right):
    return jnp.einsum('ckyxz,clyxz->kl', left, right, precision=lax.Precision.HIGHEST)

def mix_cols(values, matrix):
    return jnp.einsum('ckyxz,kl->clyxz', values, matrix, precision=lax.Precision.HIGHEST)

def inverse_factor(gram_b):
    factor = jnp.linalg.cholesky(gram_b)
    identity = jnp.eye(gram_b.shape[0], dtype=jnp.float32)
    return lax.linalg.triangular_solve(factor, identity, left_side=True, lower=True)

def face_terms(values, weights, along):
    length = values.shape[along]
    head_part = lax.slice_in_dim(values, 0, length - 1, axis=along)
    tail_part = lax.slice_in_dim(values, 1, length, axis=along)
    fluxes = lax.slice_in_dim(weights, 0, length - 1, axis=along - 2)[None, None] * (head_part - tail_part)
    pad_after = [(0, 0)] * 5
    pad_after[along] = (0, 1)
    pad_before = [(0, 0)] * 5
    pad_before[along] = (1, 0)
    return jnp.pad(fluxes, pad_after) - jnp.pad(fluxes, pad_before)

def lower_faces(weights, along):
    length = weights.shape[along]
    widths = [(0, 0)] * 3
    widths[along] = (1, 0)
    return jnp.pad(lax.slice_in_dim(weights, 0, length - 1, axis=along), widths)

def operate(values, live_x, live_y, live_z):
    return face_terms(values, live_y, 2) + face_terms(values, live_x, 3) + face_terms(values, live_z, 4)

def one_domain(start, face_x, face_y, face_z, masses, active):
    row_index = jnp.arange(NY, dtype=jnp.int32)
    plane_index = jnp.arange(NXS, dtype=jnp.int32)
    depth_index = jnp.arange(NZ, dtype=jnp.int32)
    inside = (plane_index < active)[None, :, None]
    keep_x = (plane_index + 1 < active)[None, :, None]
    keep_y = inside & (row_index + 1 < NY)[:, None, None]
    keep_z = inside & (depth_index + 1 < NZ)[None, None, :]
    live_x = face_x * keep_x.astype(jnp.float32)
    live_y = face_y * keep_y.astype(jnp.float32)
    live_z = face_z * keep_z.astype(jnp.float32)
    diagonal = live_x + lower_faces(live_x, 1) + live_y + lower_faces(live_y, 0) + live_z + lower_faces(live_z, 2) + masses
    unity = jnp.clip(jnp.minimum(plane_index + 1, active - plane_index).astype(jnp.float32) / (OV + 1), 0.0, 1.0)[None, :, None]
    b_weight = masses * unity * unity
    vectors = start * inside.astype(jnp.float32)[None, None]
    for repeat in range(STEPS):
        inv_now = inverse_factor(gram_of(vectors, b_weight[None, None] * vectors))
        ortho = mix_cols(vectors, inv_now.T)
        image = operate(ortho, live_x, live_y, live_z)
        rayleigh = gram_of(ortho, image)
        residual = image - mix_cols(b_weight[None, None] * ortho, rayleigh)
        vectors = ortho - 0.5 * residual / diagonal[None, None]
    inv_now = inverse_factor(gram_of(vectors, b_weight[None, None] * vectors))
    deflate = unity[None, None] * mix_cols(vectors, inv_now.T)
    image = operate(deflate, live_x, live_y, live_z)
    coarse = gram_of(deflate, image)
    first_planes = deflate[:, :, :, :OV]
    last_planes = lax.dynamic_slice_in_dim(image, (active - OV).astype(jnp.int32), OV, axis=3)
    return (deflate.astype(jnp.bfloat16), coarse, first_planes, last_planes)

def reference(start_vectors, face_x, face_y, face_z, masses, active):
    deflation, coarse_diag, first_planes, last_planes = lax.map(lambda packed: one_domain(*packed), (start_vectors, face_x, face_y, face_z, masses, active))
    previous = jnp.concatenate([jnp.zeros_like(last_planes[:1]), last_planes[:-1]], axis=0)
    coarse_off = jnp.einsum('sckyxz,sclyxz->skl', first_planes, previous, precision=lax.Precision.HIGHEST)
    return (deflation, coarse_diag, coarse_off)
```

```python
import functools

import jax
import jax.numpy as jnp
from jax import lax
from jax.experimental import pallas as pl
from jax.experimental.pallas import tpu as pltpu
from jax.sharding import PartitionSpec as P

OV = 4
STEPS = 2
K = 64
NX = 16
LANES = 128
SLABS = 3 * NX
GROUPS = SLABS // 4
YROWS = GROUPS * K + NX
ZROWS = 2 * K + NX
F32 = jnp.float32
BF16 = jnp.bfloat16

VM = pl.BlockSpec(memory_space=pltpu.VMEM)
SM = pl.BlockSpec(memory_space=pltpu.SMEM)
PARAMS = pltpu.CompilerParams(vmem_limit_bytes=48 << 20)

FX, FXL, FY, FYL, FZ, FZL, DINV, BW, MASS, UN = range(10)


def f32(*shape):
    return jax.ShapeDtypeStruct(shape, F32)


def lanes(rows):
    return lax.broadcasted_iota(jnp.int32, (rows, LANES), 1)


def roll(x, shift):
    if isinstance(shift, int):
        shift = shift % LANES
        return x if shift == 0 else pltpu.roll(x, shift, 1)
    return pltpu.roll(x, shift, 1)


def unity_of(plane, active):
    value = jnp.minimum(plane + 1, active - plane).astype(F32) / (OV + 1)
    return jnp.clip(value, 0.0, 1.0)


def halves(x):
    high = x.astype(BF16)
    return high, (x - high.astype(F32)).astype(BF16)


def slab(ref, index):
    return ref[pl.ds(pl.multiple_of(index * K, K), K), :]


def put(ref, index, value):
    ref[pl.ds(pl.multiple_of(index * K, K), K), :] = value


def pack_kernel(scal, v_ref, fx, fy, fz, m, p0, p1, p2, p3):
    active, px, row = scal[0], scal[1], scal[2]
    outs_ref = (p0, p1, p2, p3)
    back = ((4 - px) & 3) * 32
    block = lanes(K) >> 5

    def body(t, carry):
        c, big = t >> 2, t & 3
        outs = [None] * 4
        for xx in range(4):
            plane = big * 4 + xx
            s = v_ref[pl.ds(c * (K * NX) + plane, K, stride=NX), :]
            s = jnp.where(plane < active, s, 0.0)
            s = roll(s, back)
            for d in range(4):
                moved = roll(s, 32 * (xx - d))
                outs[d] = moved if xx == 0 else jnp.where(block == xx, moved, outs[d])
        for d in range(4):
            put(outs_ref[d], t, outs[d])
        return carry

    lax.fori_loop(0, GROUPS, body, 0)
    plane = lax.broadcasted_iota(jnp.int32, (NX, LANES), 0)
    depth = lanes(NX)
    small = depth >> 5
    inside = plane < active
    fields = (
        jnp.where(plane + 1 < active, fx[...], 0.0),
        jnp.where(inside & (row + 1 < 16), fy[...], 0.0),
        jnp.where(inside & (depth + 1 < LANES), fz[...], 0.0),
        m[...],
    )
    for d in range(4):
        out = None
        for j in range(4):
            moved = roll(roll(fields[j], back), 32 * (j - d))
            out = moved if j == 0 else jnp.where(small == j, moved, out)
        outs_ref[d][pl.ds(GROUPS * K, NX), :] = out


def edges(t, values, y_up, y_dn, z_up, z_dn):
    lane = lanes(K)
    block = lane >> 5
    up = dn = None
    for xx in range(4):
        above = roll(values[xx], 32 * (xx - 3))
        below = roll(values[xx], 32 * xx)
        up = above if xx == 0 else jnp.where(block == xx, above, up)
        dn = below if xx == 0 else jnp.where(block == xx, below, dn)
    put(y_up, t, up)
    put(y_dn, t, dn)
    c, big = t >> 2, t & 3
    group = c >> 1
    spot = (c & 1) * NX + big * 4
    high, low = slab(z_up, group), slab(z_dn, group)
    for xx in range(4):
        here = (lane & 31) == spot + xx
        high = jnp.where(here, roll(values[xx], spot + (xx + LANES - 31)), high)
        low = jnp.where(here, roll(values[xx], spot + xx), low)
    put(z_up, group, high)
    put(z_dn, group, low)


def unpack_kernel(scal, r0, r1, r2, r3, b_ref, fields, y_up, y_dn, z_up, z_dn):
    px = scal[1]
    refs = (r0, r1, r2, r3)
    block = lanes(K) >> 5
    z_up[...] = jnp.zeros_like(z_up)
    z_dn[...] = jnp.zeros_like(z_dn)

    def body(t, carry):
        got = [slab(r, t) for r in refs]
        values = []
        for xx in range(4):
            out = None
            for d in range(4):
                moved = roll(got[d], 32 * (-d - xx))
                out = moved if d == 0 else jnp.where(block == (-d) % 4, moved, out)
            out = roll(out, px * 32)
            values.append(out)
            put(b_ref, t * 4 + xx, out)
        edges(t, values, y_up, y_dn, z_up, z_dn)
        return carry

    lax.fori_loop(0, GROUPS, body, 0)
    small = lanes(NX) >> 5
    got = [r[pl.ds(GROUPS * K, NX), :] for r in refs]
    done = []
    for j in range(4):
        out = None
        for d in range(4):
            moved = roll(got[d], 32 * (-d - j))
            out = moved if d == 0 else jnp.where(small == (-d) % 4, moved, out)
        out = roll(out, px * 32)
        done.append(out)
        fields[pl.ds(j * NX, NX), :] = out
    y_up[pl.ds(GROUPS * K, NX), :] = roll(done[1], 32)
    y_dn[pl.ds(GROUPS * K, NX), :] = jnp.zeros((NX, LANES), F32)
    z_up[pl.ds(2 * K, NX), :] = roll(done[2], -31)


def line(fld, which, plane):
    return fld[pl.ds(which * NX + plane, 1), :]


def stencil(t, xx, v_ref, fld, h_up, h_dn, h_zp, h_zm):
    c, big = t >> 2, t & 3
    plane = big * 4 + xx
    at = t * 4 + xx
    lane = lanes(K)
    v = slab(v_ref, at)
    spot = (c & 1) * NX + plane
    group = c >> 1
    up = jnp.where(lane >= 96, roll(slab(h_up, t), 32 * (3 - xx)), roll(v, -32))
    dn = jnp.where(lane < 32, roll(slab(h_dn, t), -32 * xx), roll(v, 32))
    part = lane & 31
    zp = jnp.where(part == 31, roll(slab(h_zp, group), 31 - spot), roll(v, -1))
    zm = jnp.where(part == 0, roll(slab(h_zm, group), LANES - spot), roll(v, 1))
    lo = jnp.maximum(at - 1, 0)
    hi = jnp.minimum(at + 1, SLABS - 1)
    out = line(fld, FY, plane) * (v - up) + line(fld, FYL, plane) * (v - dn)
    out += line(fld, FX, plane) * (v - slab(v_ref, hi)) + line(fld, FXL, plane) * (v - slab(v_ref, lo))
    out += line(fld, FZ, plane) * (v - zp) + line(fld, FZL, plane) * (v - zm)
    return v, out


def add_gram(acc, lefts, mids, rights):
    for pair in (0, 2):
        left, right = [], []
        for xx in (pair, pair + 1):
            left.append(jnp.concatenate(halves(lefts[xx]), axis=0))
            right.append(jnp.concatenate(halves(mids[xx]) + halves(rights[xx]), axis=0))
        acc[...] += lax.dot_general(
            jnp.concatenate(left, axis=1),
            jnp.concatenate(right, axis=1),
            (((1,), (1,)), ((), ())),
            preferred_element_type=F32,
        )


def finish_gram(acc, out):
    half = acc[0:K, :] + acc[K : 2 * K, :]
    out[0:K, :] = half[:, 0:K] + half[:, K : 2 * K]
    out[K : 2 * K, :] = half[:, 2 * K : 3 * K] + half[:, 3 * K : 4 * K]


def edge_fields(fld, y_up, y_dn, z_up, z_dn):
    dinv = fld[DINV * NX : DINV * NX + NX, :]
    weight = fld[BW * NX : BW * NX + NX, :]
    lane = lanes(NX)
    y_up[pl.ds(GROUPS * K, NX), :] = jnp.where(lane < 32, roll(dinv, 32), roll(weight, 64))
    y_dn[pl.ds(GROUPS * K, NX), :] = jnp.where(lane < 32, dinv, roll(weight, 32))
    z_up[pl.ds(2 * K, NX), :] = jnp.where((lane & 31) == 0, roll(dinv, -31), roll(weight, -30))
    z_dn[pl.ds(2 * K, NX), :] = jnp.where((lane & 31) == 0, dinv, roll(weight, 1))


def first_kernel(scal, v_ref, raw, h_up, h_dn, h_zp, h_zm, av_ref, fld, grams, y_up, y_dn, z_up, z_dn, acc):
    active = scal[0]
    lane = lanes(NX)
    plane = lax.broadcasted_iota(jnp.int32, (NX, LANES), 0)
    fx, fy, fz, m = (raw[j * NX : (j + 1) * NX, :] for j in range(4))
    fxl = jnp.where(plane == 0, 0.0, pltpu.roll(fx, 1, 0))
    fyl = jnp.where(lane < 32, h_dn[GROUPS * K : GROUPS * K + NX, :], roll(fy, 32))
    fzl = jnp.where((lane & 31) == 0, h_zm[2 * K : 2 * K + NX, :], roll(fz, 1))
    dinv = 1.0 / (fx + fxl + fy + fyl + fz + fzl + m)
    u = unity_of(plane, active)
    for j, value in enumerate((fx, fxl, fy, fyl, fz, fzl, dinv, m * u * u, m, u)):
        fld[j * NX : (j + 1) * NX, :] = value
    z_up[...] = jnp.zeros_like(z_up)
    z_dn[...] = jnp.zeros_like(z_dn)
    acc[...] = jnp.zeros_like(acc)

    def body(t, carry):
        vs, bs, avs = [], [], []
        for xx in range(4):
            v, av = stencil(t, xx, v_ref, fld, h_up, h_dn, h_zp, h_zm)
            put(av_ref, t * 4 + xx, av)
            vs.append(v)
            avs.append(av)
            bs.append(v * line(fld, BW, (t & 3) * 4 + xx))
        edges(t, avs, y_up, y_dn, z_up, z_dn)
        add_gram(acc, vs, bs, avs)
        return carry

    lax.fori_loop(0, GROUPS, body, 0)
    edge_fields(fld, y_up, y_dn, z_up, z_dn)
    finish_gram(acc, grams)


def mixed(matrix, v, av, dinv, weight):
    y = v - 0.5 * (av * dinv)
    w = v * (weight * dinv)
    both = lax.dot_general(
        matrix,
        jnp.concatenate(halves(y) + halves(w), axis=0),
        (((1,), (0,)), ((), ())),
        preferred_element_type=F32,
    )
    return both[0:K, :] + both[K : 2 * K, :]


def step_kernel(last, scal, *refs):
    ins, refs = refs[:12], refs[12:]
    v_ref, av_ref, fld, mat = ins[:4]
    hv, ha = ins[4:8], ins[8:12]
    hf, refs = refs[:4], refs[4:]
    if last:
        w_ref, img_ref, grams, p0, p1, p2, p3, acc, rows_y, rows_z, n_up, n_dn, n_zp, n_zm = refs
        new_ref = w_ref
    else:
        new_ref, out_ref, grams, n_up, n_dn, n_zp, n_zm, y_up, y_dn, z_up, z_dn, acc, rows_y, rows_z = refs
    active, px = scal[0], scal[1]
    matrix = mat[...]
    one = lanes(1)
    for side in range(2):
        for big in range(4):
            for which in range(2):
                out = None
                for xx in range(4):
                    at = GROUPS * K + big * 4 + xx
                    moved = roll(hf[side][at : at + 1, :], 32 * (xx - which))
                    out = moved if xx == 0 else jnp.where((one >> 5) == xx, moved, out)
                at = (side * 4 + big) * 2 + which
                rows_y[at : at + 1, :] = out
        for which in range(2):
            out = None
            for e in range(2 * NX):
                at = 2 * K + e % NX
                moved = roll(hf[2 + side][at : at + 1, :], e - which)
                out = moved if e == 0 else jnp.where((one & 31) == e, moved, out)
            at = side * 2 + which
            rows_z[at : at + 1, :] = out
    acc[...] = jnp.zeros_like(acc)

    def new_own(t, carry):
        for xx in range(4):
            plane = (t & 3) * 4 + xx
            at = t * 4 + xx
            value = mixed(matrix, slab(v_ref, at), slab(av_ref, at), line(fld, DINV, plane), line(fld, BW, plane))
            if last:
                value = value * line(fld, UN, plane)
            put(new_ref, at, value)
        return carry

    lax.fori_loop(0, GROUPS, new_own, 0)
    block = lanes(1) >> 5

    def new_side(t, carry):
        big = t & 3
        for side, target in ((0, n_up), (1, n_dn)):
            at = (side * 4 + big) * 2
            value = mixed(
                matrix, slab(hv[side], t), slab(ha[side], t), rows_y[pl.ds(at, 1), :], rows_y[pl.ds(at + 1, 1), :]
            )
            if last:
                value = value * unity_of(big * 4 + block, active)
            put(target, t, value)
        return carry

    lax.fori_loop(0, GROUPS, new_side, 0)
    for side, target in ((0, n_zp), (1, n_zm)):
        for group in range(2):
            at = side * 2
            value = mixed(
                matrix,
                slab(hv[2 + side], group),
                slab(ha[2 + side], group),
                rows_z[at : at + 1, :],
                rows_z[at + 1 : at + 2, :],
            )
            if last:
                value = value * unity_of(one & 15, active)
            put(target, group, value)

    if not last:
        z_up[...] = jnp.zeros_like(z_up)
        z_dn[...] = jnp.zeros_like(z_dn)
    outs_ref = (p0, p1, p2, p3) if last else ()
    back = ((4 - px) & 3) * 32
    wide = lanes(K) >> 5

    def body(t, carry):
        vs, bs, avs = [], [], []
        for xx in range(4):
            plane = (t & 3) * 4 + xx
            v, av = stencil(t, xx, new_ref, fld, n_up, n_dn, n_zp, n_zm)
            vs.append(v)
            avs.append(av)
            bs.append(v * line(fld, MASS if last else BW, plane))
            if not last:
                put(out_ref, t * 4 + xx, av)
            else:
                place = plane - (active - OV)

                @pl.when((place >= 0) & (place < OV))
                def _():
                    put(img_ref, (t >> 2) * OV + place, av)

        if last:
            outs = [None] * 4
            for xx in range(4):
                s = roll(vs[xx], back)
                for d in range(4):
                    moved = roll(s, 32 * (xx - d))
                    outs[d] = moved if xx == 0 else jnp.where(wide == xx, moved, outs[d])
            for d in range(4):
                put(outs_ref[d], t, outs[d])
        else:
            edges(t, avs, y_up, y_dn, z_up, z_dn)
        add_gram(acc, vs, bs, avs)
        return carry

    lax.fori_loop(0, GROUPS, body, 0)
    finish_gram(acc, grams)


def small_dot(a, b, dims=((1,), (0,))):
    return lax.dot_general(a, b, (dims, ((), ())), precision=lax.Precision.HIGHEST, preferred_element_type=F32)


def inverse_factor(gram):
    row = lax.broadcasted_iota(jnp.int32, (8, LANES), 0)
    lane = lanes(8)
    parts = []
    for g in range(8):
        left = jnp.concatenate([gram[g * 8 : g * 8 + 8, :], jnp.zeros((8, K), F32)], axis=1)
        parts.append(jnp.where(lane == row + (g * 8 + K), 1.0, left))
    pivots = [None] * 8
    for j in range(K):
        g0, s0 = j // 8, j % 8
        pivot_row = jnp.broadcast_to(parts[g0][s0 : s0 + 1, :], (8, LANES))
        pivot = jnp.broadcast_to(pivot_row[:, j : j + 1], (8, LANES))
        scaled = pivot_row * (1.0 / pivot)
        pivots[g0] = pivot if s0 == 0 else jnp.where(row == s0, pivot, pivots[g0])
        for g in range(g0, 8):
            column = jnp.broadcast_to(parts[g][:, j : j + 1], (8, LANES))
            if g == g0:
                column = jnp.where(row > s0, column, 0.0)
            parts[g] = parts[g] - column * scaled
    return jnp.concatenate([(parts[g] * lax.rsqrt(pivots[g]))[:, K:] for g in range(8)], axis=0)


def matrix_kernel(grams, mat):
    factor = inverse_factor(grams[0:K, :])
    image = small_dot(factor, grams[K : 2 * K, :])
    rayleigh = small_dot(image, factor, ((1,), (1,)))
    other = 0.5 * small_dot(rayleigh, factor, ((0,), (0,)))
    fh, fl = halves(factor)
    oh, ol = halves(other)
    mat[...] = jnp.concatenate(
        [jnp.concatenate([fh, fh, oh, oh], axis=1), jnp.concatenate([fl, fl, ol, ol], axis=1)], axis=0
    )


def factor_kernel(grams, factor_ref, diag_ref):
    factor = inverse_factor(grams[0:K, :])
    factor_ref[...] = factor
    image = small_dot(factor, grams[K : 2 * K, :])
    diag_ref[...] = small_dot(image, factor, ((1,), (1,)))


def cross_kernel(factor, other, raw, out):
    out[...] = small_dot(small_dot(factor[...], raw[...]), other[...], ((1,), (1,)))


def off_kernel(w_ref, img_ref, out):
    acc = jnp.zeros((2 * K, 2 * K), F32)
    for c in range(3):
        for pair in (0, 2):
            left, right = [], []
            for j in (pair, pair + 1):
                left.append(jnp.concatenate(halves(slab(w_ref, c * NX + j)), axis=0))
                right.append(jnp.concatenate(halves(slab(img_ref, c * OV + j)), axis=0))
            acc += lax.dot_general(
                jnp.concatenate(left, axis=1),
                jnp.concatenate(right, axis=1),
                (((1,), (1,)), ((), ())),
                preferred_element_type=F32,
            )
    half = acc[0:K, :] + acc[K : 2 * K, :]
    out[...] = half[:, 0:K] + half[:, K : 2 * K]


def out_kernel(scal, factor, r0, r1, r2, r3, out_ref, hold):
    px = scal[1]
    refs = (r0, r1, r2, r3)
    block = lanes(K) >> 5
    fh, fl = halves(factor[...])
    matrix = jnp.concatenate([jnp.concatenate([fh, fh], axis=1), jnp.concatenate([fl, fl], axis=1)], axis=0)

    def body(t, carry):
        c, big = t >> 2, t & 3
        got = [slab(r, t) for r in refs]
        for xx in range(4):
            out = None
            for d in range(4):
                moved = roll(got[d], 32 * (-d - xx))
                out = moved if d == 0 else jnp.where(block == (-d) % 4, moved, out)
            out = roll(out, px * 32)
            both = lax.dot_general(
                matrix, jnp.concatenate(halves(out), axis=0), (((1,), (0,)), ((), ())), preferred_element_type=F32
            )
            hold[pl.ds(c * (K * NX) + big * 4 + xx, K, stride=NX), :] = both[0:K, :] + both[K : 2 * K, :]
        return carry

    lax.fori_loop(0, GROUPS, body, 0)

    def cast(i, carry):
        at = pl.ds(pl.multiple_of(i * 128, 128), 128)
        out_ref[at, :] = hold[at, :].astype(BF16)
        return carry

    lax.fori_loop(0, 3 * K * NX // 128, cast, 0)


def call(kernel, n_in, shapes, scratch=(), first=VM, name=None):
    return pl.pallas_call(
        kernel,
        out_shape=shapes,
        in_specs=[first] + [VM] * (n_in - 1),
        out_specs=jax.tree.map(lambda _: VM, shapes),
        scratch_shapes=list(scratch),
        compiler_params=PARAMS,
        name=name,
    )


def shift_x(value, d):
    return lax.ppermute(value, "dom", [(i, (i & 12) + ((i + d) & 3)) for i in range(16)])


def halo(y_up, y_dn, z_up, z_dn):
    h_dn = lax.ppermute(y_up, "dom", [(i, i + 4) for i in range(12)])
    h_up = lax.ppermute(y_dn, "dom", [(i + 4, i) for i in range(12)])
    h_zm = lax.ppermute(z_up, "dom", [(i, i + 1) for i in range(16) if i & 3 < 3])
    h_zp = lax.ppermute(z_dn, "dom", [(i + 1, i) for i in range(16) if i & 3 < 3])
    return h_up, h_dn, h_zp, h_zm


def total(value):
    for near in ((1, 0, 3, 2), (3, 2, 1, 0)):
        value = value + lax.ppermute(value, "dom", [(i, (i & 12) + near[i & 3]) for i in range(16)])
    for near in ((1, 0, 3, 2), (3, 2, 1, 0)):
        value = value + lax.ppermute(value, "dom", [(i, near[i >> 2] * 4 + (i & 3)) for i in range(16)])
    return value


def on_device(start_vectors, face_x, face_y, face_z, masses, active):
    row = lax.axis_index("dom").astype(jnp.int32)
    scal = jnp.stack([active[0], row & 3, row]).astype(jnp.int32)
    start = start_vectors.reshape(3 * K * NX, LANES)
    fields = [f.reshape(NX, LANES) for f in (face_x, face_y, face_z, masses)]
    msg = f32(YROWS, LANES)
    zmsg = f32(ZROWS, LANES)
    whole = f32(SLABS * K, LANES)
    gram2 = f32(2 * K, K)
    rows4 = (msg,) * 4
    side4 = (msg, msg, zmsg, zmsg)
    packed = call(pack_kernel, 6, rows4, first=SM, name="pack")(scal, start, *fields)
    got = [packed[0]] + [shift_x(packed[d], d) for d in (1, 2, 3)]
    v, raw, *side = call(unpack_kernel, 5, (whole, f32(4 * NX, LANES)) + side4, first=SM, name="unpack")(scal, *got)
    hv = halo(*side)
    acc = pltpu.VMEM((2 * K, 4 * K), F32)
    av, fld, grams, *side = call(
        first_kernel, 7, (whole, f32(10 * NX, LANES), gram2) + side4, (acc,), first=SM, name="first"
    )(scal, v, raw, *hv)
    ha = halo(*side)
    hf = ha
    mat_shape = jax.ShapeDtypeStruct((2 * K, 4 * K), BF16)
    rows = (pltpu.VMEM((16, LANES), F32), pltpu.VMEM((8, LANES), F32))
    for repeat in range(STEPS):
        mat = call(matrix_kernel, 1, mat_shape, name="matrix")(total(grams))
        ops = (scal, v, av, fld, mat, *hv, *ha, *hf)
        if repeat + 1 < STEPS:
            v, av, grams, *rest = call(
                functools.partial(step_kernel, False),
                17,
                (whole, whole, gram2) + side4 + side4,
                (acc,) + rows,
                first=SM,
                name="step",
            )(*ops)
            hv = tuple(rest[:4])
            ha = halo(*rest[4:])
        else:
            w, img, grams, *packed = call(
                functools.partial(step_kernel, True),
                17,
                (whole, f32(3 * OV * K, LANES), gram2) + rows4,
                (acc,) + rows + (pltpu.VMEM((YROWS, LANES), F32),) * 2 + (pltpu.VMEM((ZROWS, LANES), F32),) * 2,
                first=SM,
                name="last",
            )(*ops)
    got = [packed[0]] + [shift_x(packed[d], d) for d in (1, 2, 3)]
    behind = [(i, i + 1) for i in range(15)]
    before = lax.ppermute(img, "sub", behind)
    raw_off = call(off_kernel, 2, f32(K, K), name="off")(w, before)
    factor, diag = call(factor_kernel, 1, (f32(K, K), f32(K, K)), name="factor")(total(grams))
    off = call(cross_kernel, 3, f32(K, K), name="cross")(factor, lax.ppermute(factor, "sub", behind), total(raw_off))
    out = call(
        out_kernel,
        6,
        jax.ShapeDtypeStruct((3 * K * NX, LANES), BF16),
        (pltpu.VMEM((3 * K * NX, LANES), F32),),
        first=SM,
        name="rows",
    )(scal, factor, *got)
    return (out.reshape(1, 3, K, 1, NX, LANES), diag[None], off[None])


def solution(mesh):
    placed = (
        P("sub", None, None, "dom", None, None),
        P("sub", "dom", None, None),
        P("sub", "dom", None, None),
        P("sub", "dom", None, None),
        P("sub", "dom", None, None),
        P("sub"),
    )
    return jax.shard_map(
        on_device,
        mesh=mesh,
        in_specs=placed,
        out_specs=(
            P("sub", None, None, "dom", None, None),
            P("sub", None, None),
            P("sub", None, None),
        ),
        check_vma=False,
    )
```

```python
import functools

import jax
import jax.numpy as jnp
from jax import lax
from jax.experimental import pallas as pl
from jax.experimental.pallas import tpu as pltpu
from jax.sharding import PartitionSpec as P

OV = 4
STEPS = 2
K = 64
NX = 16
LANES = 128
SLABS = 3 * NX
GROUPS = SLABS // 4
YROWS = GROUPS * K + NX
ZROWS = 2 * K + NX
F32 = jnp.float32
BF16 = jnp.bfloat16

VM = pl.BlockSpec(memory_space=pltpu.VMEM)
SM = pl.BlockSpec(memory_space=pltpu.SMEM)
PARAMS = pltpu.CompilerParams(vmem_limit_bytes=20 << 20)

FX, FXL, FY, FYL, FZ, FZL, DINV, BW, MASS, UN = range(10)


def f32(*shape):
    return jax.ShapeDtypeStruct(shape, F32)


def lanes(rows):
    return lax.broadcasted_iota(jnp.int32, (rows, LANES), 1)


def roll(x, shift):
    if isinstance(shift, int):
        shift = shift % LANES
        return x if shift == 0 else pltpu.roll(x, shift, 1)
    return pltpu.roll(x, shift, 1)


def unity_of(plane, active):
    value = jnp.minimum(plane + 1, active - plane).astype(F32) / (OV + 1)
    return jnp.clip(value, 0.0, 1.0)


def halves(x):
    high = x.astype(BF16)
    return high, (x - high.astype(F32)).astype(BF16)


def slab(ref, index):
    return ref[pl.ds(pl.multiple_of(index * K, K), K), :]


def put(ref, index, value):
    ref[pl.ds(pl.multiple_of(index * K, K), K), :] = value


def pack_kernel(scal, v_hbm, fx_hbm, fy_hbm, fz_hbm, m_hbm, p0, p1, p2, p3, v_ref, fx, fy, fz, m, v_sem, f_sem):
    active, px, row = scal[0], scal[1], scal[2]
    whole = K * NX

    def v_copy(c):
        return pltpu.make_async_copy(v_hbm.at[pl.ds(c * whole, whole), :], v_ref.at[pl.ds(c * whole, whole), :], v_sem.at[c])

    for c in range(3):
        v_copy(c).start()
    copies = [
        pltpu.make_async_copy(src, dst, f_sem.at[j])
        for j, (src, dst) in enumerate(((fx_hbm, fx), (fy_hbm, fy), (fz_hbm, fz), (m_hbm, m)))
    ]
    for copy in copies:
        copy.start()
    outs_ref = (p0, p1, p2, p3)
    back = ((4 - px) & 3) * 32
    block = lanes(K) >> 5

    def body(t, carry):
        c, big = t >> 2, t & 3
        outs = [None] * 4
        for xx in range(4):
            plane = big * 4 + xx
            s = v_ref[pl.ds(c * (K * NX) + plane, K, stride=NX), :]
            s = jnp.where(plane < active, s, 0.0)
            s = roll(s, back)
            for d in range(4):
                moved = roll(s, 32 * (xx - d))
                outs[d] = moved if xx == 0 else jnp.where(block == xx, moved, outs[d])
        for d in range(4):
            put(outs_ref[d], t, outs[d])
        return carry

    for c in range(3):
        v_copy(c).wait()
        lax.fori_loop(c * 4, c * 4 + 4, body, 0)
    for copy in copies:
        copy.wait()
    plane = lax.broadcasted_iota(jnp.int32, (NX, LANES), 0)
    depth = lanes(NX)
    small = depth >> 5
    inside = plane < active
    fields = (
        jnp.where(plane + 1 < active, fx[...], 0.0),
        jnp.where(inside & (row + 1 < 16), fy[...], 0.0),
        jnp.where(inside & (depth + 1 < LANES), fz[...], 0.0),
        m[...],
    )
    for d in range(4):
        out = None
        for j in range(4):
            moved = roll(roll(fields[j], back), 32 * (j - d))
            out = moved if j == 0 else jnp.where(small == j, moved, out)
        outs_ref[d][pl.ds(GROUPS * K, NX), :] = out


def edges(t, values, y_up, y_dn, z_up, z_dn):
    lane = lanes(K)
    block = lane >> 5
    up = dn = None
    for xx in range(4):
        above = roll(values[xx], 32 * (xx - 3))
        below = roll(values[xx], 32 * xx)
        up = above if xx == 0 else jnp.where(block == xx, above, up)
        dn = below if xx == 0 else jnp.where(block == xx, below, dn)
    put(y_up, t, up)
    put(y_dn, t, dn)
    c, big = t >> 2, t & 3
    group = c >> 1
    spot = (c & 1) * NX + big * 4
    high, low = slab(z_up, group), slab(z_dn, group)
    for xx in range(4):
        here = (lane & 31) == spot + xx
        high = jnp.where(here, roll(values[xx], spot + (xx + LANES - 31)), high)
        low = jnp.where(here, roll(values[xx], spot + xx), low)
    put(z_up, group, high)
    put(z_dn, group, low)


def unpack_kernel(scal, r0, r1, r2, r3, b_ref, fields, y_up, y_dn, near, far, z_up, z_dn):
    px = scal[1]
    refs = (r0, r1, r2, r3)
    block = lanes(K) >> 5
    z_up[...] = jnp.zeros_like(z_up)
    z_dn[...] = jnp.zeros_like(z_dn)

    def body(t, carry):
        got = [slab(r, t) for r in refs]
        values = []
        for xx in range(4):
            out = None
            for d in range(4):
                moved = roll(got[d], 32 * (-d - xx))
                out = moved if d == 0 else jnp.where(block == (-d) % 4, moved, out)
            out = roll(out, px * 32)
            values.append(out)
            put(b_ref, t * 4 + xx, out)
        edges(t, values, y_up, y_dn, z_up, z_dn)
        return carry

    lax.fori_loop(0, GROUPS, body, 0)
    small = lanes(NX) >> 5
    got = [r[pl.ds(GROUPS * K, NX), :] for r in refs]
    done = []
    for j in range(4):
        out = None
        for d in range(4):
            moved = roll(got[d], 32 * (-d - j))
            out = moved if d == 0 else jnp.where(small == (-d) % 4, moved, out)
        out = roll(out, px * 32)
        done.append(out)
        fields[pl.ds(j * NX, NX), :] = out
    y_up[pl.ds(GROUPS * K, NX), :] = roll(done[1], 32)
    y_dn[pl.ds(GROUPS * K, NX), :] = jnp.zeros((NX, LANES), F32)
    z_up[pl.ds(2 * K, NX), :] = roll(done[2], -31)
    by_parity(scal, near, far, z_up, z_dn)


def line(fld, which, plane):
    return fld[pl.ds(which * NX + plane, 1), :]


def stencil(t, xx, v_ref, fld, h_up, h_dn, h_zp, h_zm):
    c, big = t >> 2, t & 3
    plane = big * 4 + xx
    at = t * 4 + xx
    lane = lanes(K)
    v = slab(v_ref, at)
    spot = (c & 1) * NX + plane
    group = c >> 1
    up = jnp.where(lane >= 96, roll(slab(h_up, t), 32 * (3 - xx)), roll(v, -32))
    dn = jnp.where(lane < 32, roll(slab(h_dn, t), -32 * xx), roll(v, 32))
    part = lane & 31
    zp = jnp.where(part == 31, roll(slab(h_zp, group), 31 - spot), roll(v, -1))
    zm = jnp.where(part == 0, roll(slab(h_zm, group), LANES - spot), roll(v, 1))
    lo = jnp.maximum(at - 1, 0)
    hi = jnp.minimum(at + 1, SLABS - 1)
    out = line(fld, FY, plane) * (v - up) + line(fld, FYL, plane) * (v - dn)
    out += line(fld, FX, plane) * (v - slab(v_ref, hi)) + line(fld, FXL, plane) * (v - slab(v_ref, lo))
    out += line(fld, FZ, plane) * (v - zp) + line(fld, FZL, plane) * (v - zm)
    return v, out


def add_gram(acc, lefts, mids, rights):
    for pair in (0, 2):
        left, right = [], []
        for xx in (pair, pair + 1):
            left.append(jnp.concatenate(halves(lefts[xx]), axis=0))
            right.append(jnp.concatenate(halves(mids[xx]) + halves(rights[xx]), axis=0))
        acc[...] += lax.dot_general(
            jnp.concatenate(left, axis=1),
            jnp.concatenate(right, axis=1),
            (((1,), (1,)), ((), ())),
            preferred_element_type=F32,
        )


def by_parity(scal, near, far, z_up, z_dn):
    odd = (scal[1] & 1) == 1
    up, dn = z_up[...], z_dn[...]
    near[...] = jnp.where(odd, dn, up)
    far[...] = jnp.where(odd, up, dn)


def finish_gram(acc, out):
    half = acc[0:K, :] + acc[K : 2 * K, :]
    out[0:K, 0:K] = half[:, 0:K] + half[:, K : 2 * K]
    out[0:K, K : 2 * K] = half[:, 2 * K : 3 * K] + half[:, 3 * K : 4 * K]


def edge_fields(fld, y_up, y_dn, z_up, z_dn):
    dinv = fld[DINV * NX : DINV * NX + NX, :]
    weight = fld[BW * NX : BW * NX + NX, :]
    lane = lanes(NX)
    y_up[pl.ds(GROUPS * K, NX), :] = jnp.where(lane < 32, roll(dinv, 32), roll(weight, 64))
    y_dn[pl.ds(GROUPS * K, NX), :] = jnp.where(lane < 32, dinv, roll(weight, 32))
    z_up[pl.ds(2 * K, NX), :] = jnp.where((lane & 31) == 0, roll(dinv, -31), roll(weight, -30))
    z_dn[pl.ds(2 * K, NX), :] = jnp.where((lane & 31) == 0, dinv, roll(weight, 1))


def split_near(scal, h_near, h_far, h_zp, h_zm):
    odd = (scal[1] & 1) == 1
    one = h_near[pl.ds(h_near.shape[0] - ZROWS, ZROWS), :]
    two = h_far[pl.ds(h_far.shape[0] - ZROWS, ZROWS), :]
    h_zp[...] = jnp.where(odd, two, one)
    h_zm[...] = jnp.where(odd, one, two)


def first_kernel(
    scal, v_ref, raw, h_up, h_dn, h_near, h_far, av_ref, fld, near, far, y_up, y_dn, acc, z_up, z_dn, h_zp, h_zm
):
    split_near(scal, h_near, h_far, h_zp, h_zm)
    active = scal[0]
    lane = lanes(NX)
    plane = lax.broadcasted_iota(jnp.int32, (NX, LANES), 0)
    fx, fy, fz, m = (raw[j * NX : (j + 1) * NX, :] for j in range(4))
    fxl = jnp.where(plane == 0, 0.0, pltpu.roll(fx, 1, 0))
    fyl = jnp.where(lane < 32, h_dn[GROUPS * K : GROUPS * K + NX, :], roll(fy, 32))
    fzl = jnp.where((lane & 31) == 0, h_zm[2 * K : 2 * K + NX, :], roll(fz, 1))
    dinv = 1.0 / (fx + fxl + fy + fyl + fz + fzl + m)
    u = unity_of(plane, active)
    for j, value in enumerate((fx, fxl, fy, fyl, fz, fzl, dinv, m * u * u, m, u)):
        fld[j * NX : (j + 1) * NX, :] = value
    z_up[...] = jnp.zeros_like(z_up)
    z_dn[...] = jnp.zeros_like(z_dn)
    acc[...] = jnp.zeros_like(acc)

    def body(t, carry):
        vs, bs, avs = [], [], []
        for xx in range(4):
            v, av = stencil(t, xx, v_ref, fld, h_up, h_dn, h_zp, h_zm)
            put(av_ref, t * 4 + xx, av)
            vs.append(v)
            avs.append(av)
            bs.append(v * line(fld, BW, (t & 3) * 4 + xx))
        edges(t, avs, y_up, y_dn, z_up, z_dn)
        add_gram(acc, vs, bs, avs)
        return carry

    lax.fori_loop(0, GROUPS, body, 0)
    edge_fields(fld, y_up, y_dn, z_up, z_dn)
    finish_gram(acc, near)
    by_parity(scal, near.at[pl.ds(K, ZROWS), :], far, z_up, z_dn)


def mixed(matrix, v, av, dinv, weight):
    y = v - 0.5 * (av * dinv)
    w = v * (weight * dinv)
    both = lax.dot_general(
        matrix,
        jnp.concatenate(halves(y) + halves(w), axis=0),
        (((1,), (0,)), ((), ())),
        preferred_element_type=F32,
    )
    return both[0:K, :] + both[K : 2 * K, :]


def step_kernel(last, scal, *refs):
    ins, refs = refs[:12], refs[12:]
    v_ref, av_ref, fld, mat = ins[:4]
    hv, ha = list(ins[4:8]), list(ins[8:12])
    if last:
        r_y, r_z, w_ref, img_ref, grams, p0, p1, p2, p3, acc, a_zp, a_zm, n_up, n_dn, n_zp, n_zm = refs
        new_ref = w_ref
        rows_y, rows_z = r_y, r_z
    else:
        (new_ref, out_ref, near, far, n_up, n_dn, n_zp, n_zm, y_up, y_dn, rows_y, rows_z) = refs[:12]
        acc, z_up, z_dn, v_zp, v_zm, a_zp, a_zm = refs[12:]
        split_near(scal, hv[2], hv[3], v_zp, v_zm)
        hv[2:] = [v_zp, v_zm]
    split_near(scal, ha[2], ha[3], a_zp, a_zm)
    ha[2:] = [a_zp, a_zm]
    active, px = scal[0], scal[1]
    matrix = mat[...]
    one = lanes(1)
    hf = ha
    for side in range(0 if last else 2):
        for big in range(4):
            for which in range(2):
                out = None
                for xx in range(4):
                    at = GROUPS * K + big * 4 + xx
                    moved = roll(hf[side][at : at + 1, :], 32 * (xx - which))
                    out = moved if xx == 0 else jnp.where((one >> 5) == xx, moved, out)
                at = (side * 4 + big) * 2 + which
                rows_y[at : at + 1, :] = out
        for which in range(2):
            out = None
            for e in range(2 * NX):
                at = 2 * K + e % NX
                moved = roll(hf[2 + side][at : at + 1, :], e - which)
                out = moved if e == 0 else jnp.where((one & 31) == e, moved, out)
            at = side * 2 + which
            rows_z[at : at + 1, :] = out
    acc[...] = jnp.zeros_like(acc)

    def new_own(t, carry):
        for xx in range(4):
            plane = (t & 3) * 4 + xx
            at = t * 4 + xx
            value = mixed(matrix, slab(v_ref, at), slab(av_ref, at), line(fld, DINV, plane), line(fld, BW, plane))
            if last:
                value = value * line(fld, UN, plane)
            put(new_ref, at, value)
        return carry

    lax.fori_loop(0, GROUPS, new_own, 0)
    block = lanes(1) >> 5

    def new_side(t, carry):
        big = t & 3
        for side, target in ((0, n_up), (1, n_dn)):
            at = (side * 4 + big) * 2
            value = mixed(
                matrix, slab(hv[side], t), slab(ha[side], t), rows_y[pl.ds(at, 1), :], rows_y[pl.ds(at + 1, 1), :]
            )
            if last:
                value = value * unity_of(big * 4 + block, active)
            put(target, t, value)
        return carry

    lax.fori_loop(0, GROUPS, new_side, 0)
    for side, target in ((0, n_zp), (1, n_zm)):
        for group in range(2):
            at = side * 2
            value = mixed(
                matrix,
                slab(hv[2 + side], group),
                slab(ha[2 + side], group),
                rows_z[at : at + 1, :],
                rows_z[at + 1 : at + 2, :],
            )
            if last:
                value = value * unity_of(one & 15, active)
            put(target, group, value)

    if not last:
        z_up[...] = jnp.zeros_like(z_up)
        z_dn[...] = jnp.zeros_like(z_dn)
    outs_ref = (p0, p1, p2, p3) if last else ()
    back = ((4 - px) & 3) * 32
    wide = lanes(K) >> 5

    def body(t, carry):
        vs, bs, avs = [], [], []
        for xx in range(4):
            plane = (t & 3) * 4 + xx
            v, av = stencil(t, xx, new_ref, fld, n_up, n_dn, n_zp, n_zm)
            vs.append(v)
            avs.append(av)
            bs.append(v * line(fld, MASS if last else BW, plane))
            if not last:
                put(out_ref, t * 4 + xx, av)
            else:
                place = plane - (active - OV)

                @pl.when((place >= 0) & (place < OV))
                def _():
                    put(img_ref, (t >> 2) * OV + place, av)

        if last:
            outs = [None] * 4
            for xx in range(4):
                s = roll(vs[xx], back)
                for d in range(4):
                    moved = roll(s, 32 * (xx - d))
                    outs[d] = moved if xx == 0 else jnp.where(wide == xx, moved, outs[d])
            for d in range(4):
                put(outs_ref[d], t, outs[d])
        else:
            edges(t, avs, y_up, y_dn, z_up, z_dn)
        add_gram(acc, vs, bs, avs)
        return carry

    lax.fori_loop(0, GROUPS, body, 0)
    if last:
        finish_gram(acc, grams)
    else:
        finish_gram(acc, near)
        by_parity(scal, near.at[pl.ds(K, ZROWS), :], far, z_up, z_dn)


def small_dot(a, b, dims=((1,), (0,))):
    return lax.dot_general(a, b, (dims, ((), ())), precision=lax.Precision.HIGHEST, preferred_element_type=F32)


def inverse_factor(gram):
    row = lax.broadcasted_iota(jnp.int32, (8, LANES), 0)
    lane = lanes(8)

    def one_row(x, at):
        return jnp.broadcast_to(x[at : at + 1, :], (8, LANES))

    def one_column(x, at):
        return jnp.broadcast_to(x[:, at : at + 1], (8, LANES))

    parts = []
    for g in range(8):
        left = jnp.concatenate([gram[g * 8 : g * 8 + 8, :], jnp.zeros((8, K), F32)], axis=1)
        parts.append(jnp.where(lane == row + (g * 8 + K), 1.0, left))
    pivots = [None] * 8
    for g0 in range(8):
        top = parts[g0]
        columns = [one_column(top, g0 * 8 + j) for j in range(8)]
        inverse, lines, ahead = [], [], []
        for j in range(8):
            pivot = one_row(columns[j], j)
            line_j = one_row(top, j)
            pivots[g0] = pivot if j == 0 else jnp.where(row == j, pivot, pivots[g0])
            inv = 1.0 / pivot
            factor = jnp.where(row > j, columns[j] * inv, 0.0)
            after = [one_row(columns[k], j) for k in range(j + 1, 8)]
            for k in range(j + 1, 8):
                columns[k] = columns[k] - factor * after[k - j - 1]
            top = top - factor * line_j
            inverse.append(inv)
            lines.append(line_j)
            ahead.append(after)
        parts[g0] = top
        for g in range(g0 + 1, 8):
            part = parts[g]
            columns = [one_column(part, g0 * 8 + j) for j in range(8)]
            for j in range(8):
                factor = columns[j] * inverse[j]
                for k in range(j + 1, 8):
                    columns[k] = columns[k] - factor * ahead[j][k - j - 1]
                part = part - factor * lines[j]
            parts[g] = part
    return jnp.concatenate([(parts[g] * lax.rsqrt(pivots[g]))[:, K:] for g in range(8)], axis=0)


def matrix_kernel(grams, mat):
    both = grams[0:K, :]
    factor = inverse_factor(both[:, 0:K])
    image = small_dot(factor, both[:, K : 2 * K])
    rayleigh = small_dot(image, factor, ((1,), (1,)))
    other = 0.5 * small_dot(rayleigh, factor, ((0,), (0,)))
    fh, fl = halves(factor)
    oh, ol = halves(other)
    mat[...] = jnp.concatenate(
        [jnp.concatenate([fh, fh, oh, oh], axis=1), jnp.concatenate([fl, fl, ol, ol], axis=1)], axis=0
    )


def factor_kernel(grams, factor_ref, diag_ref):
    both = grams[...]
    factor = inverse_factor(both[:, 0:K])
    factor_ref[...] = factor
    image = small_dot(factor, both[:, K : 2 * K])
    diag_ref[...] = small_dot(image, factor, ((1,), (1,)))


def cross_kernel(factor, other, raw, out):
    out[...] = small_dot(small_dot(factor[...], raw[...]), other[...], ((1,), (1,)))


def off_kernel(w_ref, img_ref, out):
    acc = jnp.zeros((2 * K, 2 * K), F32)
    for c in range(3):
        for pair in (0, 2):
            left, right = [], []
            for j in (pair, pair + 1):
                left.append(jnp.concatenate(halves(slab(w_ref, c * NX + j)), axis=0))
                right.append(jnp.concatenate(halves(slab(img_ref, c * OV + j)), axis=0))
            acc += lax.dot_general(
                jnp.concatenate(left, axis=1),
                jnp.concatenate(right, axis=1),
                (((1,), (1,)), ((), ())),
                preferred_element_type=F32,
            )
    half = acc[0:K, :] + acc[K : 2 * K, :]
    out[...] = half[:, 0:K] + half[:, K : 2 * K]


def out_kernel(scal, factor, r0, r1, r2, r3, out_ref, hold):
    px = scal[1]
    refs = (r0, r1, r2, r3)
    block = lanes(K) >> 5
    fh, fl = halves(factor[...])
    matrix = jnp.concatenate([jnp.concatenate([fh, fh], axis=1), jnp.concatenate([fl, fl], axis=1)], axis=0)

    def body(t, carry):
        c, big = t >> 2, t & 3
        got = [slab(r, t) for r in refs]
        for xx in range(4):
            out = None
            for d in range(4):
                moved = roll(got[d], 32 * (-d - xx))
                out = moved if d == 0 else jnp.where(block == (-d) % 4, moved, out)
            out = roll(out, px * 32)
            both = lax.dot_general(
                matrix, jnp.concatenate(halves(out), axis=0), (((1,), (0,)), ((), ())), preferred_element_type=F32
            )
            hold[pl.ds(c * (K * NX) + big * 4 + xx, K, stride=NX), :] = both[0:K, :] + both[K : 2 * K, :]
        return carry

    lax.fori_loop(0, GROUPS, body, 0)

    def cast(i, carry):
        at = pl.ds(pl.multiple_of(i * 128, 128), 128)
        out_ref[at, :] = hold[at, :].astype(BF16)
        return carry

    lax.fori_loop(0, 3 * K * NX // 128, cast, 0)


def call(kernel, n_in, shapes, scratch=(), first=VM, name=None, rest=VM):
    return pl.pallas_call(
        kernel,
        out_shape=shapes,
        in_specs=[first] + [rest] * (n_in - 1),
        out_specs=jax.tree.map(lambda _: VM, shapes),
        scratch_shapes=list(scratch),
        compiler_params=PARAMS,
        name=name,
    )


NEAR = ((1, 0, 3, 2), (3, 2, 1, 0))


def shift_x(value, d):
    return lax.ppermute(value, "dom", [(i, (i & 12) + ((i + d) & 3)) for i in range(16)])


def pair_x(value, which):
    return lax.ppermute(value, "dom", [(i, (i & 12) + NEAR[which][i & 3]) for i in range(16)])


def pair_y(value, which):
    return lax.ppermute(value, "dom", [(i, NEAR[which][i >> 2] * 4 + (i & 3)) for i in range(16)])


def halo_y(y_up, y_dn):
    h_dn = lax.ppermute(y_up, "dom", [(i, i + 4) for i in range(12)])
    h_up = lax.ppermute(y_dn, "dom", [(i + 4, i) for i in range(12)])
    return h_up, h_dn


def total_y(value):
    for which in range(2):
        value = value + pair_y(value, which)
    return value


def total_x(value):
    for which in range(2):
        value = value + pair_x(value, which)
    return value


def exchange(near, far, y_up, y_dn):
    h_up, h_dn = halo_y(y_up, y_dn)
    h_near = pair_x(near, 0)
    grams = near[0:K] + h_near[0:K]
    h_far = pair_x(jnp.concatenate([grams, far], axis=0), 1)
    grams = grams + h_far[0:K]
    return total_y(grams), (h_up, h_dn, h_near, h_far)


def on_device(start_vectors, face_x, face_y, face_z, masses, active):
    row = lax.axis_index("dom").astype(jnp.int32)
    scal = jnp.stack([active[0], row & 3, row]).astype(jnp.int32)
    start = start_vectors.reshape(3 * K * NX, LANES)
    fields = [f.reshape(NX, LANES) for f in (face_x, face_y, face_z, masses)]
    msg = f32(YROWS, LANES)
    zmsg = f32(ZROWS, LANES)
    near = f32(K + ZROWS, LANES)
    whole = f32(SLABS * K, LANES)
    plane = pltpu.VMEM((NX, LANES), F32)
    columns = pltpu.VMEM((ZROWS, LANES), F32)
    packed = call(
        pack_kernel,
        6,
        (msg,) * 4,
        (pltpu.VMEM((3 * K * NX, LANES), F32),)
        + (plane,) * 4
        + (pltpu.SemaphoreType.DMA((3,)), pltpu.SemaphoreType.DMA((4,))),
        first=SM,
        name="pack",
        rest=pl.BlockSpec(memory_space=pl.ANY),
    )(scal, start, *fields)
    got = [packed[0]] + [shift_x(packed[d], d) for d in (1, 2, 3)]
    v, raw, y_up, y_dn, z_near, z_far = call(
        unpack_kernel, 5, (whole, f32(4 * NX, LANES), msg, msg, zmsg, zmsg), (columns,) * 2, first=SM, name="unpack"
    )(scal, *got)
    hv = halo_y(y_up, y_dn) + (pair_x(z_near, 0), pair_x(z_far, 1))
    acc = pltpu.VMEM((2 * K, 4 * K), F32)
    av, fld, *sent = call(
        first_kernel,
        7,
        (whole, f32(10 * NX, LANES), near, zmsg, msg, msg),
        (acc,) + (columns,) * 4,
        first=SM,
        name="first",
    )(scal, v, raw, *hv)
    mat_shape = jax.ShapeDtypeStruct((2 * K, 4 * K), BF16)
    grams, ha = exchange(*sent)
    mat = call(matrix_kernel, 1, mat_shape, name="matrix")(grams)
    v, av, *rest = call(
        functools.partial(step_kernel, False),
        13,
        (whole, whole, near, zmsg, msg, msg, zmsg, zmsg, msg, msg, f32(16, LANES), f32(8, LANES)),
        (acc,) + (columns,) * 6,
        first=SM,
        name="step",
    )(scal, v, av, fld, mat, *hv, *ha)
    hv = tuple(rest[2:6])
    lines = tuple(rest[8:])
    grams, ha = exchange(rest[0], rest[1], rest[6], rest[7])
    mat = call(matrix_kernel, 1, mat_shape, name="matrix")(grams)
    w, img, grams, *packed = call(
        functools.partial(step_kernel, True),
        15,
        (whole, f32(3 * OV * K, LANES), f32(K, LANES)) + (f32(GROUPS * K, LANES),) * 4,
        (acc,) + (columns,) * 2 + (pltpu.VMEM((YROWS, LANES), F32),) * 2 + (columns,) * 2,
        first=SM,
        name="last",
    )(scal, v, av, fld, mat, *hv, *ha, *lines)
    behind = [(i, i + 1) for i in range(15)]
    before = lax.ppermute(img, "sub", behind)
    grams = total_x(grams)
    grams, packed = lax.optimization_barrier((grams, packed))
    got = [packed[0]] + [shift_x(packed[d], d) for d in (1, 2, 3)]
    raw_off = call(off_kernel, 2, f32(K, K), name="off")(w, before)
    factor, diag = call(factor_kernel, 1, (f32(K, K), f32(K, K)), name="factor")(total_y(grams))
    raw_off = total_x(total_y(raw_off))
    off = call(cross_kernel, 3, f32(K, K), name="cross")(factor, lax.ppermute(factor, "sub", behind), raw_off)
    out = call(
        out_kernel,
        6,
        jax.ShapeDtypeStruct((3 * K * NX, LANES), BF16),
        (pltpu.VMEM((3 * K * NX, LANES), F32),),
        first=SM,
        name="rows",
    )(scal, factor, *got)
    return (out.reshape(1, 3, K, 1, NX, LANES), diag[None], off[None])


def solution(mesh):
    placed = (
        P("sub", None, None, "dom", None, None),
        P("sub", "dom", None, None),
        P("sub", "dom", None, None),
        P("sub", "dom", None, None),
        P("sub", "dom", None, None),
        P("sub"),
    )
    return jax.shard_map(
        on_device,
        mesh=mesh,
        in_specs=placed,
        out_specs=(
            P("sub", None, None, "dom", None, None),
            P("sub", None, None),
            P("sub", None, None),
        ),
        check_vma=False,
    )
```

```python
import functools

import jax
import jax.numpy as jnp
from jax import lax
from jax.experimental import pallas as pl
from jax.experimental.pallas import tpu as pltpu
from jax.sharding import PartitionSpec as P


OV = 4
K = 64
NX = 16
LANES = 128
SLABS = 3 * NX
GROUPS = SLABS // 4
FROWS = GROUPS * K
YROWS = FROWS + NX
ZROWS = 3 * K + 2 * NX
F32 = jnp.float32
BF16 = jnp.bfloat16

VM = pl.BlockSpec(memory_space=pltpu.VMEM)
SM = pl.BlockSpec(memory_space=pltpu.SMEM)
PARAMS = pltpu.CompilerParams(vmem_limit_bytes=20 << 20)

FX, FXL, FY, FYL, FZ, FZL, DINV, BW, MASS, UN = range(10)


def f32(*shape):
    return jax.ShapeDtypeStruct(shape, F32)


def lanes(rows):
    return lax.broadcasted_iota(jnp.int32, (rows, LANES), 1)


def roll(x, shift):
    if isinstance(shift, int):
        shift = shift % LANES
        return x if shift == 0 else pltpu.roll(x, shift, 1)
    return pltpu.roll(x, shift, 1)


def unity_of(plane, active):
    value = jnp.minimum(plane + 1, active - plane).astype(F32) / (OV + 1)
    return jnp.clip(value, 0.0, 1.0)


def halves(x):
    high = x.astype(BF16)
    return high, (x - high.astype(F32)).astype(BF16)


def slab(ref, index):
    return ref[pl.ds(pl.multiple_of(index * K, K), K), :]


def put(ref, index, value):
    ref[pl.ds(pl.multiple_of(index * K, K), K), :] = value


def swap_blocks(v):
    block = lanes(v[0].shape[0]) >> 5
    odd, high = (block & 1) == 1, block >= 2
    w0 = jnp.where(odd, roll(v[1], 32), v[0])
    w1 = jnp.where(odd, v[1], roll(v[0], -32))
    w2 = jnp.where(odd, roll(v[3], 32), v[2])
    w3 = jnp.where(odd, v[3], roll(v[2], -32))
    return [
        jnp.where(high, roll(w2, 64), w0),
        jnp.where(high, roll(w3, 64), w1),
        jnp.where(high, w2, roll(w0, -64)),
        jnp.where(high, w3, roll(w1, -64)),
    ]


def turn(items, by):
    items = [jnp.where((by & 1) == 1, items[(i + 1) % 4], items[i]) for i in range(4)]
    return [jnp.where(by >= 2, items[(i + 2) % 4], items[i]) for i in range(4)]


def pack_kernel(scal, v_hbm, fx_hbm, fy_hbm, fz_hbm, m_hbm, p0, p1, p2, p3, v_ref, fx, fy, fz, m, v_sem, f_sem):
    active, px, row = scal[0], scal[1], scal[2]
    whole = K * NX

    def v_copy(c):
        return pltpu.make_async_copy(v_hbm.at[pl.ds(c * whole, whole), :], v_ref.at[pl.ds(c * whole, whole), :], v_sem.at[c])

    for c in range(3):
        v_copy(c).start()
    copies = [
        pltpu.make_async_copy(src, dst, f_sem.at[j])
        for j, (src, dst) in enumerate(((fx_hbm, fx), (fy_hbm, fy), (fz_hbm, fz), (m_hbm, m)))
    ]
    for copy in copies:
        copy.start()
    outs_ref = (p0, p1, p2, p3)

    def body(t, carry):
        c, big = t >> 2, t & 3
        values = []
        for xx in range(4):
            plane = big * 4 + xx
            s = v_ref[pl.ds(c * whole + plane, K, stride=NX), :]
            values.append(jnp.where(plane < active, s, 0.0))
        for d, value in enumerate(turn(swap_blocks(values), px)):
            put(outs_ref[d], t, value)
        return carry

    for c in range(3):
        v_copy(c).wait()
        lax.fori_loop(c * 4, c * 4 + 4, body, 0)
    for copy in copies:
        copy.wait()
    plane = lax.broadcasted_iota(jnp.int32, (NX, LANES), 0)
    depth = lanes(NX)
    inside = plane < active
    fx[...] = jnp.where(plane + 1 < active, fx[...], 0.0)
    fy[...] = jnp.where(inside & (row + 1 < 16), fy[...], 0.0)
    fz[...] = jnp.where(inside & (depth + 1 < LANES), fz[...], 0.0)
    for j, field in enumerate((fx, fy, fz, m)):
        values = [field[pl.ds(xx, 4, stride=4), :] for xx in range(4)]
        for d, value in enumerate(turn(swap_blocks(values), px)):
            outs_ref[d][pl.ds(FROWS + 4 * j, 4), :] = value


def edges(t, values, z_ref, base):
    part = lanes(K) & 31
    ends = None
    for r in range(4):
        moved = roll(values[r], 8 * r)
        here = (part == 8 * r) | (part == (8 * r + 31) % 32)
        ends = jnp.where(here, moved, 0.0 if r == 0 else ends)
    c, big = t >> 2, t & 3
    at = pl.ds(pl.multiple_of(base + c * K, 8), K)
    z_ref[at, :] = jnp.where(big == 0, 0.0, z_ref[at, :]) + roll(ends, big * 2)


def unpack_kernel(scal, r0, r1, r2, r3, b0, b1, b2, b3, z_ref):
    back = (4 - scal[1]) & 3
    refs = (r0, r3, r2, r1)
    outs = (b0, b1, b2, b3)

    def body(t, carry):
        values = turn([slab(r, t) for r in refs], back)
        for r in range(4):
            put(outs[r], t, values[r])
        edges(t, values, z_ref, 0)
        return carry

    lax.fori_loop(0, GROUPS, body, 0)
    values = turn([r[pl.ds(FROWS, NX), :] for r in refs], back)
    for r in range(4):
        outs[r][pl.ds(FROWS, NX), :] = values[r]
        z_ref[pl.ds(3 * K + 4 * r, 4), :] = values[r][8:12, :]
    z_ref[pl.ds(3 * K + NX, NX), :] = jnp.zeros((NX, LANES), F32)


def line(fld, which, r, big):
    return fld[pl.ds(which * NX + 4 * r + big, 1), :]


def join_columns(h_before, h_after, hz):
    before = h_before[pl.ds(h_before.shape[0] - ZROWS, ZROWS), :]
    after = h_after[pl.ds(h_after.shape[0] - ZROWS, ZROWS), :]
    hz[...] = jnp.where((lanes(ZROWS) & 1) == 0, after, roll(before, -62))


def stencils(t, v_refs, fld, h_up, h_dn, hz):
    c, big = t >> 2, t & 3
    lane = lanes(K)
    block, part = lane >> 5, lane & 31
    ends = roll(slab(hz, c), (LANES - 2 * big) & 127)
    vs = [slab(ref, t) for ref in v_refs]
    outs = []
    for r in range(4):
        v = vs[r]
        up = slab(h_up, t) if r == 3 else vs[r + 1]
        dn = slab(h_dn, t) if r == 0 else vs[r - 1]
        lo = roll(jnp.where(block == 3, slab(v_refs[r], jnp.maximum(t - 1, 0)), v), 32)
        hi = roll(jnp.where(block == 0, slab(v_refs[r], jnp.minimum(t + 1, GROUPS - 1)), v), -32)
        side = roll(ends, 31 - 8 * r)
        zp = jnp.where(part == 31, side, roll(v, -1))
        zm = jnp.where(part == 0, side, roll(v, 1))
        out = line(fld, FY, r, big) * (v - up) + line(fld, FYL, r, big) * (v - dn)
        out += line(fld, FX, r, big) * (v - hi) + line(fld, FXL, r, big) * (v - lo)
        out += line(fld, FZ, r, big) * (v - zp) + line(fld, FZL, r, big) * (v - zm)
        outs.append(out)
    return vs, outs


def add_gram(acc, lefts, mids, rights):
    for pair in (0, 2):
        left, right = [], []
        for xx in (pair, pair + 1):
            left.append(jnp.concatenate(halves(mids[xx]) + halves(rights[xx]), axis=0))
            right.append(jnp.concatenate(halves(lefts[xx]), axis=0))
        acc[...] += lax.dot_general(
            jnp.concatenate(left, axis=1),
            jnp.concatenate(right, axis=1),
            (((1,), (1,)), ((), ())),
            preferred_element_type=F32,
        )


def finish_gram(acc, out):
    half = acc[:, 0:K] + acc[:, K : 2 * K]
    out[0:K, 0:K] = half[0:K] + half[K : 2 * K]
    out[0:K, K : 2 * K] = half[2 * K : 3 * K] + half[3 * K : 4 * K]


def first_kernel(
    scal, b0, b1, b2, b3, h_up, h_dn, h_before, h_after, a0, a1, a2, a3, fld, near, hz, acc
):
    join_columns(h_before, h_after, hz)
    active = scal[0]
    v_refs, outs = (b0, b1, b2, b3), (a0, a1, a2, a3)
    lane = lanes(NX)
    row = lax.broadcasted_iota(jnp.int32, (NX, LANES), 0)
    plane = 4 * (row & 3) + (lane >> 5)
    fx, fy, fz, m = (
        jnp.concatenate([ref[FROWS + 4 * j : FROWS + 4 * j + 4, :] for ref in v_refs], axis=0) for j in range(4)
    )
    fxl = roll(jnp.where(lane >= 96, jnp.where((row & 3) == 0, 0.0, pltpu.roll(fx, 1, 0)), fx), 32)
    fyl = jnp.concatenate([h_dn[FROWS + 4 : FROWS + 8, :], fy[0:12, :]], axis=0)
    fzl = jnp.where((lane & 31) == 0, roll(hz[3 * K : 3 * K + NX, :], 31), roll(fz, 1))
    dinv = 1.0 / (fx + fxl + fy + fyl + fz + fzl + m)
    u = unity_of(plane, active)
    weight = m * u * u
    for j, value in enumerate((fx, fxl, fy, fyl, fz, fzl, dinv, weight, m, u)):
        fld[j * NX : (j + 1) * NX, :] = value
    for r in range(4):
        outs[r][pl.ds(FROWS, 4), :] = dinv[4 * r : 4 * r + 4, :]
        outs[r][pl.ds(FROWS + 4, 4), :] = weight[4 * r : 4 * r + 4, :]
        outs[r][pl.ds(FROWS + 8, 8), :] = jnp.zeros((8, LANES), F32)
    near[pl.ds(4 * K, NX), :] = dinv
    near[pl.ds(4 * K + NX, NX), :] = weight
    acc[...] = jnp.zeros_like(acc)

    def body(t, carry):
        vs, avs = stencils(t, v_refs, fld, h_up, h_dn, hz)
        for r in range(4):
            put(outs[r], t, avs[r])
        edges(t, avs, near, K)
        add_gram(acc, vs, [v * line(fld, BW, r, t & 3) for r, v in enumerate(vs)], avs)
        return carry

    lax.fori_loop(0, GROUPS, body, 0)
    finish_gram(acc, near)


def mixed(matrix, v, av, dinv, weight):
    y = v - 0.5 * (av * dinv)
    w = v * (weight * dinv)
    both = lax.dot_general(
        matrix,
        jnp.concatenate(halves(y) + halves(w), axis=0),
        (((1,), (0,)), ((), ())),
        preferred_element_type=F32,
    )
    return both[0:K, :] + both[K : 2 * K, :]


def step_kernel(last, scal, *refs):
    v_refs, a_refs = refs[0:4], refs[4:8]
    fld, mat, hv_up, hv_dn, hv_z, ha_up, ha_dn, ha_before, ha_after = refs[8:17]
    if last:
        rows, img_ref, grams = refs[17:20]
        outs_ref = refs[20:24]
        acc, ha_z, n_up, n_dn, n_z = refs[24:29]
        new_refs, image_refs = refs[29:33], refs[33:37]
    else:
        new_refs, image_refs = refs[17:21], refs[21:25]
        near, n_up, n_dn, n_z, rows, acc, ha_z = refs[25:]
    active, px = scal[0], scal[1]
    join_columns(ha_before, ha_after, ha_z)
    matrix = mat[...]
    one = lanes(1)
    if not last:
        rows[0:8, :] = ha_up[FROWS : FROWS + 8, :]
        rows[8:16, :] = ha_dn[FROWS : FROWS + 8, :]
        for which in range(2):
            out = None
            for e in range(NX):
                at = 3 * K + which * NX + e
                moved = roll(ha_z[at : at + 1, :], 2 * e)
                out = moved if e == 0 else jnp.where((one & 30) == 2 * e, moved, out)
            rows[16 + which : 17 + which, :] = out
    acc[...] = jnp.zeros_like(acc)

    def new_own(t, carry):
        big = t & 3
        for r in range(4):
            value = mixed(
                matrix, slab(v_refs[r], t), slab(a_refs[r], t), line(fld, DINV, r, big), line(fld, BW, r, big)
            )
            if last:
                value = value * line(fld, UN, r, big)
            put(new_refs[r], t, value)
        return carry

    lax.fori_loop(0, GROUPS, new_own, 0, unroll=2)
    block = one >> 5

    def new_side(t, carry):
        big = t & 3
        for start, target, hv, ha in ((0, n_up, hv_up, ha_up), (8, n_dn, hv_dn, ha_dn)):
            value = mixed(
                matrix, slab(hv, t), slab(ha, t), rows[pl.ds(start + big, 1), :], rows[pl.ds(start + 4 + big, 1), :]
            )
            if last:
                value = value * unity_of(big * 4 + block, active)
            put(target, t, value)
        return carry

    lax.fori_loop(0, GROUPS, new_side, 0, unroll=2)
    for c in range(3):
        value = mixed(matrix, slab(hv_z, c), slab(ha_z, c), rows[16:17, :], rows[17:18, :])
        if last:
            xx = jnp.where((one & 1) == 0, block, (block + 1) & 3)
            value = value * unity_of(4 * (((one & 31) >> 1) & 3) + xx, active)
        put(n_z, c, value)

    def body(t, carry):
        vs, avs = stencils(t, new_refs, fld, n_up, n_dn, n_z)
        for r in range(4):
            put(image_refs[r], t, avs[r])
        if last:
            for d, value in enumerate(turn(vs, px)):
                put(outs_ref[d], t, value)
        else:
            edges(t, avs, near, K)
        weight = MASS if last else BW
        add_gram(acc, vs, [v * line(fld, weight, r, t & 3) for r, v in enumerate(vs)], avs)
        return carry

    lax.fori_loop(0, GROUPS, body, 0)
    if last:
        finish_gram(acc, grams)
        start = active - OV
        group, skip = start >> 2, start & 3
        late = (lanes(K) >> 5) < skip
        for c in range(3):
            values = []
            for r in range(4):
                here = slab(image_refs[r], c * 4 + group)
                after = slab(image_refs[r], jnp.minimum(c * 4 + group + 1, GROUPS - 1))
                values.append(roll(jnp.where(late, after, here), ((4 - skip) & 3) * 32))
            for d, value in enumerate(turn(values, px)):
                put(img_ref, d * 3 + c, value)
    else:
        for r in range(4):
            image_refs[r][pl.ds(FROWS, NX), :] = jnp.zeros((NX, LANES), F32)
            new_refs[r][pl.ds(FROWS, NX), :] = jnp.zeros((NX, LANES), F32)
        near[pl.ds(4 * K, 2 * NX), :] = jnp.zeros((2 * NX, LANES), F32)
        finish_gram(acc, near)


def small_dot(a, b, dims=((1,), (0,))):
    return lax.dot_general(a, b, (dims, ((), ())), precision=lax.Precision.HIGHEST, preferred_element_type=F32)


def inverse_factor(gram):
    row = lax.broadcasted_iota(jnp.int32, (8, LANES), 0)
    lane = lanes(8)

    def one_row(x, at):
        return jnp.broadcast_to(x[at : at + 1, :], (8, LANES))

    def one_column(x, at):
        return jnp.broadcast_to(x[:, at : at + 1], (8, LANES))

    parts = []
    for g in range(8):
        left = jnp.concatenate([gram[g * 8 : g * 8 + 8, :], jnp.zeros((8, K), F32)], axis=1)
        parts.append(jnp.where(lane == row + (g * 8 + K), 1.0, left))
    pivots = [None] * 8
    for g0 in range(8):
        top = parts[g0]
        columns = [one_column(top, g0 * 8 + j) for j in range(8)]
        inverse, lines, ahead = [], [], []
        for j in range(8):
            pivot = one_row(columns[j], j)
            line_j = one_row(top, j)
            pivots[g0] = pivot if j == 0 else jnp.where(row == j, pivot, pivots[g0])
            inv = 1.0 / pivot
            factor = jnp.where(row > j, columns[j] * inv, 0.0)
            after = [one_row(columns[k], j) for k in range(j + 1, 8)]
            for k in range(j + 1, 8):
                columns[k] = columns[k] - factor * after[k - j - 1]
            top = top - factor * line_j
            inverse.append(inv)
            lines.append(line_j)
            ahead.append(after)
        parts[g0] = top
        for g in range(g0 + 1, 8):
            part = parts[g]
            columns = [one_column(part, g0 * 8 + j) for j in range(8)]
            for j in range(8):
                factor = columns[j] * inverse[j]
                for k in range(j + 1, 8):
                    columns[k] = columns[k] - factor * ahead[j][k - j - 1]
                part = part - factor * lines[j]
            parts[g] = part
    return jnp.concatenate([(parts[g] * lax.rsqrt(pivots[g]))[:, K:] for g in range(8)], axis=0)


def matrix_kernel(grams, mat):
    both = grams[0:K, :]
    factor = inverse_factor(both[:, 0:K])
    image = small_dot(factor, both[:, K : 2 * K], ((1,), (1,)))
    rayleigh = small_dot(image, factor, ((1,), (1,)))
    other = 0.5 * small_dot(rayleigh, factor, ((0,), (0,)))
    fh, fl = halves(factor)
    oh, ol = halves(other)
    mat[...] = jnp.concatenate(
        [jnp.concatenate([fh, fh, oh, oh], axis=1), jnp.concatenate([fl, fl, ol, ol], axis=1)], axis=0
    )


def factor_kernel(grams, factor_ref, diag_ref):
    both = grams[...]
    factor = inverse_factor(both[:, 0:K])
    factor_ref[...] = factor
    image = small_dot(factor, both[:, K : 2 * K], ((1,), (1,)))
    diag_ref[...] = small_dot(image, factor, ((1,), (1,)))


def cross_kernel(factor, other, raw, out):
    out[...] = small_dot(small_dot(factor[...], raw[:, 0:K]), other[...], ((1,), (1,)))


def off_kernel(w0, w1, w2, w3, img_ref, out):
    acc = jnp.zeros((2 * K, 2 * K), F32)
    for c in range(3):
        for pair in (0, 2):
            left, right = [], []
            for r in (pair, pair + 1):
                left.append(jnp.concatenate(halves(slab((w0, w1, w2, w3)[r], c * 4)), axis=0))
                right.append(jnp.concatenate(halves(slab(img_ref, r * 3 + c)), axis=0))
            acc += lax.dot_general(
                jnp.concatenate(left, axis=1),
                jnp.concatenate(right, axis=1),
                (((1,), (1,)), ((), ())),
                preferred_element_type=F32,
            )
    half = acc[0:K, :] + acc[K : 2 * K, :]
    out[:, 0:K] = half[:, 0:K] + half[:, K : 2 * K]
    out[:, K : 2 * K] = jnp.zeros((K, K), F32)


def out_kernel(scal, factor, r0, r1, r2, r3, out_ref, hold):
    back = (4 - scal[1]) & 3
    refs = (r0, r3, r2, r1)
    fh, fl = halves(factor[...])
    matrix = jnp.concatenate([jnp.concatenate([fh, fh], axis=1), jnp.concatenate([fl, fl], axis=1)], axis=0)

    def body(t, carry):
        c, big = t >> 2, t & 3
        values = swap_blocks(turn([slab(r, t) for r in refs], back))
        for xx in range(4):
            both = lax.dot_general(
                matrix, jnp.concatenate(halves(values[xx]), axis=0), (((1,), (0,)), ((), ())), preferred_element_type=F32
            )
            hold[pl.ds(c * (K * NX) + big * 4 + xx, K, stride=NX), :] = both[0:K, :] + both[K : 2 * K, :]
        return carry

    lax.fori_loop(0, GROUPS, body, 0)

    def cast(i, carry):
        at = pl.ds(pl.multiple_of(i * 128, 128), 128)
        out_ref[at, :] = hold[at, :].astype(BF16)
        return carry

    lax.fori_loop(0, 3 * K * NX // 128, cast, 0)


def call(kernel, n_in, shapes, scratch=(), first=VM, rest=VM, params=PARAMS):
    return pl.pallas_call(
        kernel,
        out_shape=shapes,
        in_specs=[first] + [rest] * (n_in - 1),
        out_specs=jax.tree.map(lambda _: VM, shapes),
        scratch_shapes=list(scratch),
        compiler_params=params,
    )


def shift_x(value, d):
    return lax.ppermute(value, "dom", [(i, (i & 12) + ((i + d) & 3)) for i in range(16)])


def shift_y(value, d):
    return lax.ppermute(value, "dom", [(i, (i + 4 * d) & 15) for i in range(16)])


def halo_y(y_up, y_dn):
    h_dn = lax.ppermute(y_up, "dom", [(i, i + 4) for i in range(12)])
    h_up = lax.ppermute(y_dn, "dom", [(i + 4, i) for i in range(12)])
    return h_up, h_dn


def total(value, shift):
    parts = {}
    for d in (1, 3, 2):
        parts[d] = shift(value, d)
    return (value + parts[2]) + (parts[1] + parts[3])


def to_rows(packed):
    got = [packed[0]]
    for d in (1, 2, 3):
        got.append(shift_x(packed[d], d))
    return got


def exchange(near, images):
    h_before = shift_x(near, 1)
    h_after = shift_x(near, 3)
    own = near[0:K]
    far = shift_x(own, 2)
    h_up, h_dn = halo_y(images[3], images[0])
    grams = (own + far) + (h_before[0:K] + h_after[0:K])
    return total(grams, shift_y), (h_up, h_dn, h_before, h_after)


def blocks(start_vectors, face_x, face_y, face_z, masses, active):
    row = lax.axis_index("dom").astype(jnp.int32)
    scal = jnp.stack([active[0], row & 3, row]).astype(jnp.int32)
    start = start_vectors.reshape(3 * K * NX, LANES)
    fields = [f.reshape(NX, LANES) for f in (face_x, face_y, face_z, masses)]
    msg = f32(YROWS, LANES)
    zmsg = f32(ZROWS, LANES)
    near = f32(K + ZROWS, LANES)
    plane = pltpu.VMEM((NX, LANES), F32)
    columns = pltpu.VMEM((ZROWS, LANES), F32)
    packed = call(
        pack_kernel,
        6,
        (msg,) * 4,
        (pltpu.VMEM((3 * K * NX, LANES), F32),)
        + (plane,) * 4
        + (pltpu.SemaphoreType.DMA((3,)), pltpu.SemaphoreType.DMA((4,))),
        first=SM,
        rest=pl.BlockSpec(memory_space=pl.ANY),
        params=pltpu.CompilerParams(vmem_limit_bytes=67_000_000),
    )(scal, start, *fields)
    got = to_rows(packed)
    *v, z_edge = call(unpack_kernel, 5, (msg,) * 4 + (zmsg,), first=SM)(scal, *got)
    hv = halo_y(v[3], v[0])
    h_before, h_after = shift_x(z_edge, 1), shift_x(z_edge, 3)
    acc = pltpu.VMEM((4 * K, 2 * K), F32)
    *av, fld, near_new, hv_z = call(
        first_kernel, 9, (msg,) * 4 + (f32(10 * NX, LANES), near, zmsg), (acc,), first=SM
    )(scal, *v, *hv, h_before, h_after)
    mat_shape = jax.ShapeDtypeStruct((2 * K, 4 * K), BF16)
    grams, ha = exchange(near_new, av)
    mat = call(matrix_kernel, 1, mat_shape)(grams)
    out = call(
        functools.partial(step_kernel, False),
        18,
        (msg,) * 8 + (near, msg, msg, zmsg, f32(24, LANES)),
        (acc, columns),
        first=SM,
    )(scal, *v, *av, fld, mat, *hv, hv_z, *ha)
    v, av, (near_new, n_up, n_dn, n_z, rows) = out[:4], out[4:8], out[8:]
    grams, ha = exchange(near_new, av)
    mat = call(matrix_kernel, 1, mat_shape)(grams)
    side = pltpu.VMEM((YROWS, LANES), F32)
    part = f32(FROWS, LANES)
    img, grams, *packed = call(
        functools.partial(step_kernel, True),
        19,
        (part, f32(K, LANES)) + (part,) * 4,
        (acc, columns, side, side, columns) + (side,) * 8,
        first=SM,
    )(scal, *v, *av, fld, mat, n_up, n_dn, n_z, *ha, rows)
    behind = [(i, i + 1) for i in range(15)]
    before = lax.ppermute(img, "sub", behind)
    got = to_rows(packed)
    raw_off = call(off_kernel, 5, f32(K, 2 * K))(*packed, before)
    both = jnp.concatenate([grams, raw_off], axis=0)
    both = total(total(both, shift_y), shift_x)
    factor, diag = call(factor_kernel, 1, (f32(K, K), f32(K, K)))(both[0:K])
    other = lax.ppermute(factor, "sub", behind)
    off = call(cross_kernel, 3, f32(K, K))(factor, other, both[K:])
    out = call(
        out_kernel,
        6,
        jax.ShapeDtypeStruct((3 * K * NX, LANES), BF16),
        (pltpu.VMEM((3 * K * NX, LANES), F32),),
        first=SM,
    )(scal, factor, *got)
    return (out.reshape(1, 3, K, 1, NX, LANES), diag[None], off[None])


def solution(mesh):
    placed = (
        P("sub", None, None, "dom", None, None),
        P("sub", "dom", None, None),
        P("sub", "dom", None, None),
        P("sub", "dom", None, None),
        P("sub", "dom", None, None),
        P("sub"),
    )
    return jax.shard_map(
        blocks,
        mesh=mesh,
        in_specs=placed,
        out_specs=(
            P("sub", None, None, "dom", None, None),
            P("sub", None, None),
            P("sub", None, None),
        ),
        check_vma=False,
    )
```

```python
import functools

import jax
import jax.numpy as jnp
from jax import lax
from jax.experimental import pallas as pl
from jax.experimental.pallas import tpu as pltpu
from jax.sharding import PartitionSpec as P


OV = 4
K = 64
NX = 16
LANES = 128
SLABS = 3 * NX
GROUPS = SLABS // 4
FROWS = GROUPS * K
YROWS = FROWS + NX
ZROWS = 3 * K + 2 * NX
F32 = jnp.float32
BF16 = jnp.bfloat16

VM = pl.BlockSpec(memory_space=pltpu.VMEM)
SM = pl.BlockSpec(memory_space=pltpu.SMEM)
PARAMS = pltpu.CompilerParams(vmem_limit_bytes=20 << 20)

FX, FXL, FY, FYL, FZ, FZL, DINV, BW, MASS, UN = range(10)


def f32(*shape):
    return jax.ShapeDtypeStruct(shape, F32)


def lanes(rows):
    return lax.broadcasted_iota(jnp.int32, (rows, LANES), 1)


def roll(x, shift):
    if isinstance(shift, int):
        shift = shift % LANES
        return x if shift == 0 else pltpu.roll(x, shift, 1)
    return pltpu.roll(x, shift, 1)


def unity_of(plane, active):
    value = jnp.minimum(plane + 1, active - plane).astype(F32) / (OV + 1)
    return jnp.clip(value, 0.0, 1.0)


def halves(x):
    high = x.astype(BF16)
    return high, (x - high.astype(F32)).astype(BF16)


def slab(ref, index):
    return ref[pl.ds(pl.multiple_of(index * K, K), K), :]


def put(ref, index, value):
    ref[pl.ds(pl.multiple_of(index * K, K), K), :] = value


def swap_blocks(v):
    block = lanes(v[0].shape[0]) >> 5
    odd, high = (block & 1) == 1, block >= 2
    w0 = jnp.where(odd, roll(v[1], 32), v[0])
    w1 = jnp.where(odd, v[1], roll(v[0], -32))
    w2 = jnp.where(odd, roll(v[3], 32), v[2])
    w3 = jnp.where(odd, v[3], roll(v[2], -32))
    return [
        jnp.where(high, roll(w2, 64), w0),
        jnp.where(high, roll(w3, 64), w1),
        jnp.where(high, w2, roll(w0, -64)),
        jnp.where(high, w3, roll(w1, -64)),
    ]


def turn(items, by):
    items = [jnp.where((by & 1) == 1, items[(i + 1) % 4], items[i]) for i in range(4)]
    return [jnp.where(by >= 2, items[(i + 2) % 4], items[i]) for i in range(4)]


def pack_kernel(scal, v_hbm, fx_hbm, fy_hbm, fz_hbm, m_hbm, p0, p1, p2, p3, v_ref, fx, fy, fz, m, v_sem, f_sem):
    active, px, row = scal[0], scal[1], scal[2]
    whole = K * NX

    def v_copy(c):
        return pltpu.make_async_copy(v_hbm.at[pl.ds(c * whole, whole), :], v_ref.at[pl.ds(c * whole, whole), :], v_sem.at[c])

    for c in range(3):
        v_copy(c).start()
    copies = [
        pltpu.make_async_copy(src, dst, f_sem.at[j])
        for j, (src, dst) in enumerate(((fx_hbm, fx), (fy_hbm, fy), (fz_hbm, fz), (m_hbm, m)))
    ]
    for copy in copies:
        copy.start()
    outs_ref = (p0, p1, p2, p3)

    def body(t, carry):
        c, big = t >> 2, t & 3
        values = []
        for xx in range(4):
            plane = big * 4 + xx
            s = v_ref[pl.ds(c * whole + plane, K, stride=NX), :]
            values.append(jnp.where(plane < active, s, 0.0))
        for d, value in enumerate(turn(swap_blocks(values), px)):
            put(outs_ref[d], t, value)
        return carry

    for c in range(3):
        v_copy(c).wait()
        lax.fori_loop(c * 4, c * 4 + 4, body, 0)
    for copy in copies:
        copy.wait()
    plane = lax.broadcasted_iota(jnp.int32, (NX, LANES), 0)
    depth = lanes(NX)
    inside = plane < active
    fx[...] = jnp.where(plane + 1 < active, fx[...], 0.0)
    fy[...] = jnp.where(inside & (row + 1 < 16), fy[...], 0.0)
    fz[...] = jnp.where(inside & (depth + 1 < LANES), fz[...], 0.0)
    for j, field in enumerate((fx, fy, fz, m)):
        values = [field[pl.ds(xx, 4, stride=4), :] for xx in range(4)]
        for d, value in enumerate(turn(swap_blocks(values), px)):
            outs_ref[d][pl.ds(FROWS + 4 * j, 4), :] = value


def edges(t, values, z_ref, base):
    part = lanes(K) & 31
    ends = None
    for r in range(4):
        moved = roll(values[r], 8 * r)
        here = (part == 8 * r) | (part == (8 * r + 31) % 32)
        ends = jnp.where(here, moved, 0.0 if r == 0 else ends)
    c, big = t >> 2, t & 3
    at = pl.ds(pl.multiple_of(base + c * K, 8), K)
    z_ref[at, :] = jnp.where(big == 0, 0.0, z_ref[at, :]) + roll(ends, big * 2)


def unpack_kernel(scal, r0, r1, r2, r3, b0, b1, b2, b3, z_ref):
    back = (4 - scal[1]) & 3
    refs = (r0, r3, r2, r1)
    outs = (b0, b1, b2, b3)

    def body(t, carry):
        values = turn([slab(r, t) for r in refs], back)
        for r in range(4):
            put(outs[r], t, values[r])
        edges(t, values, z_ref, 0)
        return carry

    lax.fori_loop(0, GROUPS, body, 0)
    values = turn([r[pl.ds(FROWS, NX), :] for r in refs], back)
    for r in range(4):
        outs[r][pl.ds(FROWS, NX), :] = values[r]
        z_ref[pl.ds(3 * K + 4 * r, 4), :] = values[r][8:12, :]
    z_ref[pl.ds(3 * K + NX, NX), :] = jnp.zeros((NX, LANES), F32)


def line(fld, which, r, big):
    return fld[pl.ds(which * NX + 4 * r + big, 1), :]


def join_columns(h_before, h_after, hz):
    before = h_before[pl.ds(h_before.shape[0] - ZROWS, ZROWS), :]
    after = h_after[pl.ds(h_after.shape[0] - ZROWS, ZROWS), :]
    hz[...] = jnp.where((lanes(ZROWS) & 1) == 0, after, roll(before, -62))


def stencils(t, v_refs, fld, h_up, h_dn, hz):
    c, big = t >> 2, t & 3
    lane = lanes(K)
    block, part = lane >> 5, lane & 31
    ends = roll(slab(hz, c), (LANES - 2 * big) & 127)
    vs = [slab(ref, t) for ref in v_refs]
    outs = []
    for r in range(4):
        v = vs[r]
        up = slab(h_up, t) if r == 3 else vs[r + 1]
        dn = slab(h_dn, t) if r == 0 else vs[r - 1]
        lo = roll(jnp.where(block == 3, slab(v_refs[r], jnp.maximum(t - 1, 0)), v), 32)
        hi = roll(jnp.where(block == 0, slab(v_refs[r], jnp.minimum(t + 1, GROUPS - 1)), v), -32)
        side = roll(ends, 31 - 8 * r)
        zp = jnp.where(part == 31, side, roll(v, -1))
        zm = jnp.where(part == 0, side, roll(v, 1))
        out = line(fld, FY, r, big) * (v - up) + line(fld, FYL, r, big) * (v - dn)
        out += line(fld, FX, r, big) * (v - hi) + line(fld, FXL, r, big) * (v - lo)
        out += line(fld, FZ, r, big) * (v - zp) + line(fld, FZL, r, big) * (v - zm)
        outs.append(out)
    return vs, outs


def add_gram(acc, lefts, mids, rights):
    for pair in (0, 2):
        left, right = [], []
        for xx in (pair, pair + 1):
            left.append(jnp.concatenate(halves(mids[xx]) + halves(rights[xx]), axis=0))
            right.append(jnp.concatenate(halves(lefts[xx]), axis=0))
        acc[...] += lax.dot_general(
            jnp.concatenate(left, axis=1),
            jnp.concatenate(right, axis=1),
            (((1,), (1,)), ((), ())),
            preferred_element_type=F32,
        )


def finish_gram(acc, out):
    half = acc[:, 0:K] + acc[:, K : 2 * K]
    out[0:K, 0:K] = half[0:K] + half[K : 2 * K]
    out[0:K, K : 2 * K] = half[2 * K : 3 * K] + half[3 * K : 4 * K]


def first_kernel(
    scal, b0, b1, b2, b3, h_up, h_dn, h_before, h_after, a0, a1, a2, a3, fld, near, hz, acc
):
    join_columns(h_before, h_after, hz)
    active = scal[0]
    v_refs, outs = (b0, b1, b2, b3), (a0, a1, a2, a3)
    lane = lanes(NX)
    row = lax.broadcasted_iota(jnp.int32, (NX, LANES), 0)
    plane = 4 * (row & 3) + (lane >> 5)
    fx, fy, fz, m = (
        jnp.concatenate([ref[FROWS + 4 * j : FROWS + 4 * j + 4, :] for ref in v_refs], axis=0) for j in range(4)
    )
    fxl = roll(jnp.where(lane >= 96, jnp.where((row & 3) == 0, 0.0, pltpu.roll(fx, 1, 0)), fx), 32)
    fyl = jnp.concatenate([h_dn[FROWS + 4 : FROWS + 8, :], fy[0:12, :]], axis=0)
    fzl = jnp.where((lane & 31) == 0, roll(hz[3 * K : 3 * K + NX, :], 31), roll(fz, 1))
    dinv = 1.0 / (fx + fxl + fy + fyl + fz + fzl + m)
    u = unity_of(plane, active)
    weight = m * u * u
    for j, value in enumerate((fx, fxl, fy, fyl, fz, fzl, dinv, weight, m, u)):
        fld[j * NX : (j + 1) * NX, :] = value
    for r in range(4):
        outs[r][pl.ds(FROWS, 4), :] = dinv[4 * r : 4 * r + 4, :]
        outs[r][pl.ds(FROWS + 4, 4), :] = weight[4 * r : 4 * r + 4, :]
        outs[r][pl.ds(FROWS + 8, 8), :] = jnp.zeros((8, LANES), F32)
    near[pl.ds(4 * K, NX), :] = dinv
    near[pl.ds(4 * K + NX, NX), :] = weight
    acc[...] = jnp.zeros_like(acc)

    def body(t, carry):
        vs, avs = stencils(t, v_refs, fld, h_up, h_dn, hz)
        for r in range(4):
            put(outs[r], t, avs[r])
        edges(t, avs, near, K)
        add_gram(acc, vs, [v * line(fld, BW, r, t & 3) for r, v in enumerate(vs)], avs)
        return carry

    lax.fori_loop(0, GROUPS, body, 0)
    finish_gram(acc, near)


def mixed(matrix, v, av, dinv, weight):
    y = v - 0.5 * (av * dinv)
    w = v * (weight * dinv)
    both = lax.dot_general(
        matrix,
        jnp.concatenate(halves(y) + halves(w), axis=0),
        (((1,), (0,)), ((), ())),
        preferred_element_type=F32,
    )
    return both[0:K, :] + both[K : 2 * K, :]


def step_kernel(last, scal, *refs):
    v_refs, a_refs = refs[0:4], refs[4:8]
    fld, mat, hv_up, hv_dn, hv_z, ha_up, ha_dn, ha_before, ha_after = refs[8:17]
    if last:
        rows, img_ref, grams = refs[17:20]
        outs_ref = refs[20:24]
        acc, ha_z, n_up, n_dn, n_z = refs[24:29]
        new_refs, image_refs = refs[29:33], refs[33:37]
    else:
        new_refs, image_refs = refs[17:21], refs[21:25]
        near, n_up, n_dn, n_z, rows, acc, ha_z = refs[25:]
    active, px = scal[0], scal[1]
    join_columns(ha_before, ha_after, ha_z)
    matrix = mat[...]
    one = lanes(1)
    if not last:
        rows[0:8, :] = ha_up[FROWS : FROWS + 8, :]
        rows[8:16, :] = ha_dn[FROWS : FROWS + 8, :]
        for which in range(2):
            out = None
            for e in range(NX):
                at = 3 * K + which * NX + e
                moved = roll(ha_z[at : at + 1, :], 2 * e)
                out = moved if e == 0 else jnp.where((one & 30) == 2 * e, moved, out)
            rows[16 + which : 17 + which, :] = out
    acc[...] = jnp.zeros_like(acc)

    def new_own(t, carry):
        big = t & 3
        for r in range(4):
            value = mixed(
                matrix, slab(v_refs[r], t), slab(a_refs[r], t), line(fld, DINV, r, big), line(fld, BW, r, big)
            )
            if last:
                value = value * line(fld, UN, r, big)
            put(new_refs[r], t, value)
        return carry

    lax.fori_loop(0, GROUPS, new_own, 0, unroll=2)
    block = one >> 5

    def new_side(t, carry):
        big = t & 3
        for start, target, hv, ha in ((0, n_up, hv_up, ha_up), (8, n_dn, hv_dn, ha_dn)):
            value = mixed(
                matrix, slab(hv, t), slab(ha, t), rows[pl.ds(start + big, 1), :], rows[pl.ds(start + 4 + big, 1), :]
            )
            if last:
                value = value * unity_of(big * 4 + block, active)
            put(target, t, value)
        return carry

    lax.fori_loop(0, GROUPS, new_side, 0, unroll=2)
    for c in range(3):
        value = mixed(matrix, slab(hv_z, c), slab(ha_z, c), rows[16:17, :], rows[17:18, :])
        if last:
            xx = jnp.where((one & 1) == 0, block, (block + 1) & 3)
            value = value * unity_of(4 * (((one & 31) >> 1) & 3) + xx, active)
        put(n_z, c, value)

    def body(t, carry):
        vs, avs = stencils(t, new_refs, fld, n_up, n_dn, n_z)
        for r in range(4):
            put(image_refs[r], t, avs[r])
        if last:
            for d, value in enumerate(turn(vs, px)):
                put(outs_ref[d], t, value)
        else:
            edges(t, avs, near, K)
        weight = MASS if last else BW
        add_gram(acc, vs, [v * line(fld, weight, r, t & 3) for r, v in enumerate(vs)], avs)
        return carry

    lax.fori_loop(0, GROUPS, body, 0)
    if last:
        finish_gram(acc, grams)
        img_ref[pl.ds(FROWS, K), :] = grams[...]
        start = active - OV
        group, skip = start >> 2, start & 3
        late = (lanes(K) >> 5) < skip
        for c in range(3):
            values = []
            for r in range(4):
                here = slab(image_refs[r], c * 4 + group)
                after = slab(image_refs[r], jnp.minimum(c * 4 + group + 1, GROUPS - 1))
                values.append(roll(jnp.where(late, after, here), ((4 - skip) & 3) * 32))
            for d, value in enumerate(turn(values, px)):
                put(img_ref, d * 3 + c, value)
    else:
        for r in range(4):
            image_refs[r][pl.ds(FROWS, NX), :] = jnp.zeros((NX, LANES), F32)
            new_refs[r][pl.ds(FROWS, NX), :] = jnp.zeros((NX, LANES), F32)
        near[pl.ds(4 * K, 2 * NX), :] = jnp.zeros((2 * NX, LANES), F32)
        finish_gram(acc, near)


def small_dot(a, b, dims=((1,), (0,))):
    return lax.dot_general(a, b, (dims, ((), ())), precision=lax.Precision.HIGHEST, preferred_element_type=F32)


def inverse_factor(gram):
    row = lax.broadcasted_iota(jnp.int32, (8, LANES), 0)
    lane = lanes(8)

    def one_row(x, at):
        return jnp.broadcast_to(x[at : at + 1, :], (8, LANES))

    def one_column(x, at):
        return jnp.broadcast_to(x[:, at : at + 1], (8, LANES))

    parts = []
    for g in range(8):
        left = jnp.concatenate([gram[g * 8 : g * 8 + 8, :], jnp.zeros((8, K), F32)], axis=1)
        parts.append(jnp.where(lane == row + (g * 8 + K), 1.0, left))
    pivots = [None] * 8
    for g0 in range(8):
        top = parts[g0]
        columns = [one_column(top, g0 * 8 + j) for j in range(8)]
        inverse, lines, ahead = [], [], []
        for j in range(8):
            pivot = one_row(columns[j], j)
            line_j = one_row(top, j)
            pivots[g0] = pivot if j == 0 else jnp.where(row == j, pivot, pivots[g0])
            inv = 1.0 / pivot
            factor = jnp.where(row > j, columns[j] * inv, 0.0)
            after = [one_row(columns[k], j) for k in range(j + 1, 8)]
            for k in range(j + 1, 8):
                columns[k] = columns[k] - factor * after[k - j - 1]
            top = top - factor * line_j
            inverse.append(inv)
            lines.append(line_j)
            ahead.append(after)
        parts[g0] = top
        for g in range(g0 + 1, 8):
            part = parts[g]
            columns = [one_column(part, g0 * 8 + j) for j in range(8)]
            for j in range(8):
                factor = columns[j] * inverse[j]
                for k in range(j + 1, 8):
                    columns[k] = columns[k] - factor * ahead[j][k - j - 1]
                part = part - factor * lines[j]
            parts[g] = part
    return jnp.concatenate([(parts[g] * lax.rsqrt(pivots[g]))[:, K:] for g in range(8)], axis=0)


def matrix_kernel(grams, mat):
    both = grams[0:K, :]
    factor = inverse_factor(both[:, 0:K])
    image = small_dot(factor, both[:, K : 2 * K], ((1,), (1,)))
    rayleigh = small_dot(image, factor, ((1,), (1,)))
    other = 0.5 * small_dot(rayleigh, factor, ((0,), (0,)))
    fh, fl = halves(factor)
    oh, ol = halves(other)
    mat[...] = jnp.concatenate(
        [jnp.concatenate([fh, fh, oh, oh], axis=1), jnp.concatenate([fl, fl, ol, ol], axis=1)], axis=0
    )


def off_kernel(w0, w1, w2, w3, img_ref, out):
    acc = jnp.zeros((2 * K, 2 * K), F32)
    for c in range(3):
        for pair in (0, 2):
            left, right = [], []
            for r in (pair, pair + 1):
                left.append(jnp.concatenate(halves(slab((w0, w1, w2, w3)[r], c * 4)), axis=0))
                right.append(jnp.concatenate(halves(slab(img_ref, r * 3 + c)), axis=0))
            acc += lax.dot_general(
                jnp.concatenate(left, axis=1),
                jnp.concatenate(right, axis=1),
                (((1,), (1,)), ((), ())),
                preferred_element_type=F32,
            )
    half = acc[0:K, :] + acc[K : 2 * K, :]
    out[:, 0:K] = half[:, 0:K] + half[:, K : 2 * K]
    before = pltpu.roll(img_ref[pl.ds(FROWS, K), :], K, 1)
    out[:, K : 2 * K] = before[:, K : 2 * K]


def out_kernel(scal, both, r0, r1, r2, r3, out_hbm, diag_ref, off_ref, hold, cast, sem):
    back = (4 - scal[1]) & 3
    refs = (r0, r3, r2, r1)
    gram = both[0:K, :]
    raw = both[K : 2 * K, :]
    row = lax.broadcasted_iota(jnp.int32, (K, K), 0)
    column = lax.broadcasted_iota(jnp.int32, (K, K), 1)
    before = jnp.where(scal[3] == 0, (row == column).astype(F32), raw[:, K : 2 * K])
    factor = inverse_factor(gram[:, 0:K])
    other = inverse_factor(before)
    image = small_dot(factor, gram[:, K : 2 * K], ((1,), (1,)))
    diag_ref[...] = small_dot(image, factor, ((1,), (1,)))
    off_ref[...] = small_dot(small_dot(factor, raw[:, 0:K]), other, ((1,), (1,)))
    fh, fl = halves(factor)
    matrix = jnp.concatenate([jnp.concatenate([fh, fh], axis=1), jnp.concatenate([fl, fl], axis=1)], axis=0)
    whole = K * NX

    def body(t, carry):
        c, big = t >> 2, t & 3
        values = swap_blocks(turn([slab(r, t) for r in refs], back))
        for xx in range(4):
            mix = lax.dot_general(
                matrix, jnp.concatenate(halves(values[xx]), axis=0), (((1,), (0,)), ((), ())), preferred_element_type=F32
            )
            hold[pl.ds(c * whole + big * 4 + xx, K, stride=NX), :] = mix[0:K, :] + mix[K : 2 * K, :]
        return carry

    def to_bf16(i, carry):
        at = pl.ds(pl.multiple_of(i * 128, 128), 128)
        cast[at, :] = hold[at, :].astype(BF16)
        return carry

    def copy(c):
        at = pl.ds(c * whole, whole)
        return pltpu.make_async_copy(cast.at[at, :], out_hbm.at[at, :], sem.at[c])

    for c in range(3):
        lax.fori_loop(4 * c, 4 * c + 4, body, 0)
        lax.fori_loop(c * (whole // 128), (c + 1) * (whole // 128), to_bf16, 0)
        copy(c).start()
    for c in range(3):
        copy(c).wait()


def call(kernel, n_in, shapes, scratch=(), first=VM, rest=VM, params=PARAMS):
    return pl.pallas_call(
        kernel,
        out_shape=shapes,
        in_specs=[first] + [rest] * (n_in - 1),
        out_specs=jax.tree.map(lambda _: VM, shapes),
        scratch_shapes=list(scratch),
        compiler_params=params,
    )


def shift_x(value, d):
    return lax.ppermute(value, "dom", [(i, (i & 12) + ((i + d) & 3)) for i in range(16)])


def shift_y(value, d):
    return lax.ppermute(value, "dom", [(i, (i + 4 * d) & 15) for i in range(16)])


def halo_y(y_up, y_dn):
    h_dn = lax.ppermute(y_up, "dom", [(i, i + 4) for i in range(12)])
    h_up = lax.ppermute(y_dn, "dom", [(i + 4, i) for i in range(12)])
    return h_up, h_dn


def total(value, shift):
    parts = {}
    for d in (1, 3, 2):
        parts[d] = shift(value, d)
    return (value + parts[2]) + (parts[1] + parts[3])


def to_rows(packed):
    got = [packed[0]]
    for d in (1, 2, 3):
        got.append(shift_x(packed[d], d))
    return got


def exchange(near, images):
    own = total(near[0:K], shift_y)
    h_up, h_dn = halo_y(images[3], images[0])
    near = jnp.concatenate([own, near[K:]], axis=0)
    h_before = shift_x(near, 1)
    h_after = shift_x(near, 3)
    far = shift_x(own, 2)
    grams = (own + far) + (h_before[0:K] + h_after[0:K])
    return grams, (h_up, h_dn, h_before, h_after)


def blocks(start_vectors, face_x, face_y, face_z, masses, active):
    row = lax.axis_index("dom").astype(jnp.int32)
    scal = jnp.stack([active[0], row & 3, row, lax.axis_index("sub").astype(jnp.int32)]).astype(jnp.int32)
    start = start_vectors.reshape(3 * K * NX, LANES)
    fields = [f.reshape(NX, LANES) for f in (face_x, face_y, face_z, masses)]
    msg = f32(YROWS, LANES)
    zmsg = f32(ZROWS, LANES)
    near = f32(K + ZROWS, LANES)
    plane = pltpu.VMEM((NX, LANES), F32)
    columns = pltpu.VMEM((ZROWS, LANES), F32)
    packed = call(
        pack_kernel,
        6,
        (msg,) * 4,
        (pltpu.VMEM((3 * K * NX, LANES), F32),)
        + (plane,) * 4
        + (pltpu.SemaphoreType.DMA((3,)), pltpu.SemaphoreType.DMA((4,))),
        first=SM,
        rest=pl.BlockSpec(memory_space=pl.ANY),
        params=pltpu.CompilerParams(vmem_limit_bytes=67_000_000),
    )(scal, start, *fields)
    got = to_rows(packed)
    *v, z_edge = call(unpack_kernel, 5, (msg,) * 4 + (zmsg,), first=SM)(scal, *got)
    hv = halo_y(v[3], v[0])
    h_before, h_after = shift_x(z_edge, 1), shift_x(z_edge, 3)
    acc = pltpu.VMEM((4 * K, 2 * K), F32)
    *av, fld, near_new, hv_z = call(
        first_kernel, 9, (msg,) * 4 + (f32(10 * NX, LANES), near, zmsg), (acc,), first=SM
    )(scal, *v, *hv, h_before, h_after)
    mat_shape = jax.ShapeDtypeStruct((2 * K, 4 * K), BF16)
    grams, ha = exchange(near_new, av)
    mat = call(matrix_kernel, 1, mat_shape)(grams)
    out = call(
        functools.partial(step_kernel, False),
        18,
        (msg,) * 8 + (near, msg, msg, zmsg, f32(24, LANES)),
        (acc, columns),
        first=SM,
    )(scal, *v, *av, fld, mat, *hv, hv_z, *ha)
    v, av, (near_new, n_up, n_dn, n_z, rows) = out[:4], out[4:8], out[8:]
    grams, ha = exchange(near_new, av)
    mat = call(matrix_kernel, 1, mat_shape)(grams)
    side = pltpu.VMEM((YROWS, LANES), F32)
    part = f32(FROWS, LANES)
    img, grams, *packed = call(
        functools.partial(step_kernel, True),
        19,
        (f32(FROWS + K, LANES), f32(K, LANES)) + (part,) * 4,
        (acc, columns, side, side, columns) + (side,) * 8,
        first=SM,
    )(scal, *v, *av, fld, mat, n_up, n_dn, n_z, *ha, rows)
    behind = [(i, i + 1) for i in range(15)]
    before = lax.ppermute(img, "sub", behind)
    got = to_rows(packed)
    raw_off = call(off_kernel, 5, f32(K, 2 * K))(*packed, before)
    both = jnp.concatenate([grams, raw_off], axis=0)
    both = total(total(both, shift_y), shift_x)
    hbm = pl.BlockSpec(memory_space=pl.ANY)
    out, diag, off = pl.pallas_call(
        out_kernel,
        out_shape=(jax.ShapeDtypeStruct((3 * K * NX, LANES), BF16), f32(K, K), f32(K, K)),
        in_specs=[SM] + [VM] * 5,
        out_specs=(hbm, VM, VM),
        scratch_shapes=[
            pltpu.VMEM((3 * K * NX, LANES), F32),
            pltpu.VMEM((3 * K * NX, LANES), BF16),
            pltpu.SemaphoreType.DMA((3,)),
        ],
        compiler_params=PARAMS,
        name="rows",
    )(scal, both, *got)
    return (out.reshape(1, 3, K, 1, NX, LANES), diag[None], off[None])


def solution(mesh):
    placed = (
        P("sub", None, None, "dom", None, None),
        P("sub", "dom", None, None),
        P("sub", "dom", None, None),
        P("sub", "dom", None, None),
        P("sub", "dom", None, None),
        P("sub"),
    )
    return jax.shard_map(
        blocks,
        mesh=mesh,
        in_specs=placed,
        out_specs=(
            P("sub", None, None, "dom", None, None),
            P("sub", None, None),
            P("sub", None, None),
        ),
        check_vma=False,
    )
```

```python
import functools

import jax
import jax.numpy as jnp
from jax import lax
from jax.experimental import pallas as pl
from jax.experimental.pallas import tpu as pltpu
from jax.sharding import PartitionSpec as P


OV = 4
K = 64
NX = 16
LANES = 128
SLABS = 3 * NX
GROUPS = SLABS // 4
FROWS = GROUPS * K
YROWS = FROWS + NX
AROWS = 4 * K
BROWS = 8 * K
ZROWS = 3 * K + 2 * NX
F32 = jnp.float32
BF16 = jnp.bfloat16

VM = pl.BlockSpec(memory_space=pltpu.VMEM)
SM = pl.BlockSpec(memory_space=pltpu.SMEM)
PARAMS = pltpu.CompilerParams(vmem_limit_bytes=20 << 20)

FX, FXL, FY, FYL, FZ, FZL, DINV, BW, MASS, UN = range(10)


def f32(*shape):
    return jax.ShapeDtypeStruct(shape, F32)


def lanes(rows):
    return lax.broadcasted_iota(jnp.int32, (rows, LANES), 1)


def roll(x, shift):
    if isinstance(shift, int):
        shift = shift % LANES
        return x if shift == 0 else pltpu.roll(x, shift, 1)
    return pltpu.roll(x, shift, 1)


def unity_of(plane, active):
    value = jnp.minimum(plane + 1, active - plane).astype(F32) / (OV + 1)
    return jnp.clip(value, 0.0, 1.0)


def halves(x):
    high = x.astype(BF16)
    return high, (x - high.astype(F32)).astype(BF16)


def slab(ref, index):
    return ref[pl.ds(pl.multiple_of(index * K, K), K), :]


def put(ref, index, value):
    ref[pl.ds(pl.multiple_of(index * K, K), K), :] = value


def swap_blocks(v):
    block = lanes(v[0].shape[0]) >> 5
    odd, high = (block & 1) == 1, block >= 2
    w0 = jnp.where(odd, roll(v[1], 32), v[0])
    w1 = jnp.where(odd, v[1], roll(v[0], -32))
    w2 = jnp.where(odd, roll(v[3], 32), v[2])
    w3 = jnp.where(odd, v[3], roll(v[2], -32))
    return [
        jnp.where(high, roll(w2, 64), w0),
        jnp.where(high, roll(w3, 64), w1),
        jnp.where(high, w2, roll(w0, -64)),
        jnp.where(high, w3, roll(w1, -64)),
    ]


def turn(items, by):
    items = [jnp.where((by & 1) == 1, items[(i + 1) % 4], items[i]) for i in range(4)]
    return [jnp.where(by >= 2, items[(i + 2) % 4], items[i]) for i in range(4)]


def pack_rows(t, c, v_ref, active, px, outs_ref):
    big = t & 3
    values = []
    for xx in range(4):
        plane = big * 4 + xx
        s = v_ref[pl.ds(c * (K * NX) + plane, K, stride=NX), :]
        values.append(jnp.where(plane < active, s, 0.0))
    for d, value in enumerate(turn(swap_blocks(values), px)):
        put(outs_ref[d], t, value)


def pack_a_kernel(scal, v_hbm, fx_hbm, fy_hbm, fz_hbm, m_hbm, p0, p1, p2, p3, v_ref, fx, fy, fz, m, v_sem, f_sem):
    active, px, row = scal[0], scal[1], scal[2]
    outs_ref = (p0, p1, p2, p3)
    v_copy = pltpu.make_async_copy(v_hbm.at[pl.ds(0, K * NX), :], v_ref, v_sem.at[0])
    v_copy.start()
    copies = [
        pltpu.make_async_copy(src, dst, f_sem.at[j])
        for j, (src, dst) in enumerate(((fx_hbm, fx), (fy_hbm, fy), (fz_hbm, fz), (m_hbm, m)))
    ]
    for copy in copies:
        copy.start()
    for copy in copies:
        copy.wait()
    plane = lax.broadcasted_iota(jnp.int32, (NX, LANES), 0)
    depth = lanes(NX)
    inside = plane < active
    fx[...] = jnp.where(plane + 1 < active, fx[...], 0.0)
    fy[...] = jnp.where(inside & (row + 1 < 16), fy[...], 0.0)
    fz[...] = jnp.where(inside & (depth + 1 < LANES), fz[...], 0.0)
    for j, field in enumerate((fx, fy, fz, m)):
        values = [field[pl.ds(xx, 4, stride=4), :] for xx in range(4)]
        for d, value in enumerate(turn(swap_blocks(values), px)):
            outs_ref[d][pl.ds(AROWS + 4 * j, 4), :] = value
    v_copy.wait()

    def body(t, carry):
        pack_rows(t, 0, v_ref, active, px, outs_ref)
        return carry

    lax.fori_loop(0, 4, body, 0)


def pack_b_kernel(scal, v_hbm, p0, p1, p2, p3, v_ref, v_sem):
    active, px = scal[0], scal[1]
    whole = K * NX

    def v_copy(c):
        return pltpu.make_async_copy(v_hbm.at[pl.ds((c + 1) * whole, whole), :], v_ref.at[pl.ds(c * whole, whole), :], v_sem.at[c])

    def body(t, carry):
        pack_rows(t, t >> 2, v_ref, active, px, (p0, p1, p2, p3))
        return carry

    for c in range(2):
        v_copy(c).start()
    for c in range(2):
        v_copy(c).wait()
        lax.fori_loop(4 * c, 4 * c + 4, body, 0)


def edges(t, values, z_ref, base):
    part = lanes(K) & 31
    ends = None
    for r in range(4):
        moved = roll(values[r], 8 * r)
        here = (part == 8 * r) | (part == (8 * r + 31) % 32)
        ends = jnp.where(here, moved, 0.0 if r == 0 else ends)
    c, big = t >> 2, t & 3
    at = pl.ds(pl.multiple_of(base + c * K, 8), K)
    z_ref[at, :] = jnp.where(big == 0, 0.0, z_ref[at, :]) + roll(ends, big * 2)


def unpack_a_kernel(scal, r0, r1, r2, r3, b0, b1, b2, b3, z_ref):
    back = (4 - scal[1]) & 3
    refs = (r0, r3, r2, r1)
    outs = (b0, b1, b2, b3)

    def body(t, carry):
        values = turn([slab(r, t) for r in refs], back)
        for r in range(4):
            put(outs[r], t, values[r])
        edges(t, values, z_ref, 0)
        return carry

    lax.fori_loop(0, 4, body, 0)
    values = turn([r[pl.ds(AROWS, NX), :] for r in refs], back)
    for r in range(4):
        outs[r][pl.ds(AROWS, NX), :] = values[r]
        z_ref[pl.ds(K + 4 * r, 4), :] = values[r][8:12, :]


def unpack_b_kernel(scal, r0, r1, r2, r3, e0, e1, e2, e3, za_ref, b0, b1, b2, b3, c0, c1, z_ref):
    back = (4 - scal[1]) & 3
    refs = (r0, r3, r2, r1)
    outs = (b0, b1, b2, b3)
    for r, early in enumerate((e0, e1, e2, e3)):
        outs[r][0:AROWS, :] = early[0:AROWS, :]
        outs[r][FROWS:YROWS, :] = early[AROWS : AROWS + NX, :]
    z_ref[0:K, :] = za_ref[0:K, :]
    z_ref[pl.ds(3 * K, NX), :] = za_ref[pl.ds(K, NX), :]
    z_ref[pl.ds(3 * K + NX, NX), :] = jnp.zeros((NX, LANES), F32)

    def body(t, carry):
        values = turn([slab(r, t) for r in refs], back)
        for r in range(4):
            put(outs[r], t + 4, values[r])
        put(c0, t, values[0])
        put(c1, t, values[3])
        edges(t + 4, values, z_ref, 0)
        return carry

    lax.fori_loop(0, 8, body, 0)


def line(fld, which, r, big):
    return fld[pl.ds(which * NX + 4 * r + big, 1), :]


def join_columns(h_before, h_after, hz):
    before = h_before[pl.ds(h_before.shape[0] - ZROWS, ZROWS), :]
    after = h_after[pl.ds(h_after.shape[0] - ZROWS, ZROWS), :]
    hz[...] = jnp.where((lanes(ZROWS) & 1) == 0, after, roll(before, -62))


def stencils(t, v_refs, fld, h_up, h_dn, hz):
    c, big = t >> 2, t & 3
    lane = lanes(K)
    block, part = lane >> 5, lane & 31
    ends = roll(slab(hz, c), (LANES - 2 * big) & 127)
    vs = [slab(ref, t) for ref in v_refs]
    outs = []
    for r in range(4):
        v = vs[r]
        up = slab(h_up, t) if r == 3 else vs[r + 1]
        dn = slab(h_dn, t) if r == 0 else vs[r - 1]
        lo = roll(jnp.where(block == 3, slab(v_refs[r], jnp.maximum(t - 1, 0)), v), 32)
        hi = roll(jnp.where(block == 0, slab(v_refs[r], jnp.minimum(t + 1, GROUPS - 1)), v), -32)
        side = roll(ends, 31 - 8 * r)
        zp = jnp.where(part == 31, side, roll(v, -1))
        zm = jnp.where(part == 0, side, roll(v, 1))
        out = line(fld, FY, r, big) * (v - up) + line(fld, FYL, r, big) * (v - dn)
        out += line(fld, FX, r, big) * (v - hi) + line(fld, FXL, r, big) * (v - lo)
        out += line(fld, FZ, r, big) * (v - zp) + line(fld, FZL, r, big) * (v - zm)
        outs.append(out)
    return vs, outs


def add_gram(acc, lefts, mids, rights):
    for pair in (0, 2):
        left, right = [], []
        for xx in (pair, pair + 1):
            left.append(jnp.concatenate(halves(mids[xx]) + halves(rights[xx]), axis=0))
            right.append(jnp.concatenate(halves(lefts[xx]), axis=0))
        acc[...] += lax.dot_general(
            jnp.concatenate(left, axis=1),
            jnp.concatenate(right, axis=1),
            (((1,), (1,)), ((), ())),
            preferred_element_type=F32,
        )


def finish_gram(acc, out):
    half = acc[:, 0:K] + acc[:, K : 2 * K]
    out[0:K, 0:K] = half[0:K] + half[K : 2 * K]
    out[0:K, K : 2 * K] = half[2 * K : 3 * K] + half[3 * K : 4 * K]


def first_kernel(
    scal, b0, b1, b2, b3, up_a, dn_a, up_b, dn_b, h_before, h_after, a0, a1, a2, a3, fld, near, hz, h_up, h_dn, acc
):
    for whole, early, late in ((h_up, up_a, up_b), (h_dn, dn_a, dn_b)):
        whole[0:AROWS, :] = early[0:AROWS, :]
        whole[AROWS:FROWS, :] = late[...]
        whole[FROWS:YROWS, :] = early[AROWS : AROWS + NX, :]
    join_columns(h_before, h_after, hz)
    active = scal[0]
    v_refs, outs = (b0, b1, b2, b3), (a0, a1, a2, a3)
    lane = lanes(NX)
    row = lax.broadcasted_iota(jnp.int32, (NX, LANES), 0)
    plane = 4 * (row & 3) + (lane >> 5)
    fx, fy, fz, m = (
        jnp.concatenate([ref[FROWS + 4 * j : FROWS + 4 * j + 4, :] for ref in v_refs], axis=0) for j in range(4)
    )
    fxl = roll(jnp.where(lane >= 96, jnp.where((row & 3) == 0, 0.0, pltpu.roll(fx, 1, 0)), fx), 32)
    fyl = jnp.concatenate([h_dn[FROWS + 4 : FROWS + 8, :], fy[0:12, :]], axis=0)
    fzl = jnp.where((lane & 31) == 0, roll(hz[3 * K : 3 * K + NX, :], 31), roll(fz, 1))
    dinv = 1.0 / (fx + fxl + fy + fyl + fz + fzl + m)
    u = unity_of(plane, active)
    weight = m * u * u
    for j, value in enumerate((fx, fxl, fy, fyl, fz, fzl, dinv, weight, m, u)):
        fld[j * NX : (j + 1) * NX, :] = value
    for r in range(4):
        outs[r][pl.ds(FROWS, 4), :] = dinv[4 * r : 4 * r + 4, :]
        outs[r][pl.ds(FROWS + 4, 4), :] = weight[4 * r : 4 * r + 4, :]
        outs[r][pl.ds(FROWS + 8, 8), :] = jnp.zeros((8, LANES), F32)
    near[pl.ds(4 * K, NX), :] = dinv
    near[pl.ds(4 * K + NX, NX), :] = weight
    acc[...] = jnp.zeros_like(acc)

    def body(t, carry):
        vs, avs = stencils(t, v_refs, fld, h_up, h_dn, hz)
        for r in range(4):
            put(outs[r], t, avs[r])
        edges(t, avs, near, K)
        add_gram(acc, vs, [v * line(fld, BW, r, t & 3) for r, v in enumerate(vs)], avs)
        return carry

    lax.fori_loop(0, GROUPS, body, 0)
    finish_gram(acc, near)


def mixed(matrix, v, av, dinv, weight):
    y = v - 0.5 * (av * dinv)
    w = v * (weight * dinv)
    both = lax.dot_general(
        matrix,
        jnp.concatenate(halves(y) + halves(w), axis=0),
        (((1,), (0,)), ((), ())),
        preferred_element_type=F32,
    )
    return both[0:K, :] + both[K : 2 * K, :]


def step_kernel(last, scal, *refs):
    v_refs, a_refs = refs[0:4], refs[4:8]
    fld, mat, hv_up, hv_dn, hv_z, ha_up, ha_dn, ha_before, ha_after = refs[8:17]
    if last:
        rows, img_ref, grams = refs[17:20]
        outs_ref = refs[20:24]
        acc, ha_z, n_up, n_dn, n_z = refs[24:29]
        new_refs, image_refs = refs[29:33], refs[33:37]
    else:
        new_refs, image_refs = refs[17:21], refs[21:25]
        near, n_up, n_dn, n_z, rows, acc, ha_z = refs[25:]
    active, px = scal[0], scal[1]
    join_columns(ha_before, ha_after, ha_z)
    matrix = mat[...]
    one = lanes(1)
    if not last:
        rows[0:8, :] = ha_up[FROWS : FROWS + 8, :]
        rows[8:16, :] = ha_dn[FROWS : FROWS + 8, :]
        for which in range(2):
            out = None
            for e in range(NX):
                at = 3 * K + which * NX + e
                moved = roll(ha_z[at : at + 1, :], 2 * e)
                out = moved if e == 0 else jnp.where((one & 30) == 2 * e, moved, out)
            rows[16 + which : 17 + which, :] = out
    acc[...] = jnp.zeros_like(acc)

    def new_own(t, carry):
        big = t & 3
        for r in range(4):
            value = mixed(
                matrix, slab(v_refs[r], t), slab(a_refs[r], t), line(fld, DINV, r, big), line(fld, BW, r, big)
            )
            if last:
                value = value * line(fld, UN, r, big)
            put(new_refs[r], t, value)
        return carry

    lax.fori_loop(0, GROUPS, new_own, 0, unroll=2)
    block = one >> 5

    def new_side(t, carry):
        big = t & 3
        for start, target, hv, ha in ((0, n_up, hv_up, ha_up), (8, n_dn, hv_dn, ha_dn)):
            value = mixed(
                matrix, slab(hv, t), slab(ha, t), rows[pl.ds(start + big, 1), :], rows[pl.ds(start + 4 + big, 1), :]
            )
            if last:
                value = value * unity_of(big * 4 + block, active)
            put(target, t, value)
        return carry

    lax.fori_loop(0, GROUPS, new_side, 0, unroll=2)
    for c in range(3):
        value = mixed(matrix, slab(hv_z, c), slab(ha_z, c), rows[16:17, :], rows[17:18, :])
        if last:
            xx = jnp.where((one & 1) == 0, block, (block + 1) & 3)
            value = value * unity_of(4 * (((one & 31) >> 1) & 3) + xx, active)
        put(n_z, c, value)

    def body(t, carry):
        vs, avs = stencils(t, new_refs, fld, n_up, n_dn, n_z)
        for r in range(4):
            put(image_refs[r], t, avs[r])
        if last:
            for d, value in enumerate(turn(vs, px)):
                put(outs_ref[d], t, value)
        else:
            edges(t, avs, near, K)
        weight = MASS if last else BW
        add_gram(acc, vs, [v * line(fld, weight, r, t & 3) for r, v in enumerate(vs)], avs)
        return carry

    lax.fori_loop(0, GROUPS, body, 0)
    if last:
        finish_gram(acc, grams)
        img_ref[pl.ds(FROWS, K), :] = grams[...]
        start = active - OV
        group, skip = start >> 2, start & 3
        late = (lanes(K) >> 5) < skip
        for c in range(3):
            values = []
            for r in range(4):
                here = slab(image_refs[r], c * 4 + group)
                after = slab(image_refs[r], jnp.minimum(c * 4 + group + 1, GROUPS - 1))
                values.append(roll(jnp.where(late, after, here), ((4 - skip) & 3) * 32))
            for d, value in enumerate(turn(values, px)):
                put(img_ref, d * 3 + c, value)
    else:
        for r in range(4):
            image_refs[r][pl.ds(FROWS, NX), :] = jnp.zeros((NX, LANES), F32)
            new_refs[r][pl.ds(FROWS, NX), :] = jnp.zeros((NX, LANES), F32)
        near[pl.ds(4 * K, 2 * NX), :] = jnp.zeros((2 * NX, LANES), F32)
        finish_gram(acc, near)


def small_dot(a, b, dims=((1,), (0,))):
    return lax.dot_general(a, b, (dims, ((), ())), precision=lax.Precision.HIGHEST, preferred_element_type=F32)


def inverse_factor(gram):
    row = lax.broadcasted_iota(jnp.int32, (8, LANES), 0)
    lane = lanes(8)

    def one_row(x, at):
        return jnp.broadcast_to(x[at : at + 1, :], (8, LANES))

    def one_column(x, at):
        return jnp.broadcast_to(x[:, at : at + 1], (8, LANES))

    parts = []
    for g in range(8):
        left = jnp.concatenate([gram[g * 8 : g * 8 + 8, :], jnp.zeros((8, K), F32)], axis=1)
        parts.append(jnp.where(lane == row + (g * 8 + K), 1.0, left))
    pivots = [None] * 8
    for g0 in range(8):
        top = parts[g0]
        columns = [one_column(top, g0 * 8 + j) for j in range(8)]
        inverse, lines, ahead = [], [], []
        for j in range(8):
            pivot = one_row(columns[j], j)
            line_j = one_row(top, j)
            pivots[g0] = pivot if j == 0 else jnp.where(row == j, pivot, pivots[g0])
            inv = 1.0 / pivot
            factor = jnp.where(row > j, columns[j] * inv, 0.0)
            after = [one_row(columns[k], j) for k in range(j + 1, 8)]
            for k in range(j + 1, 8):
                columns[k] = columns[k] - factor * after[k - j - 1]
            top = top - factor * line_j
            inverse.append(inv)
            lines.append(line_j)
            ahead.append(after)
        parts[g0] = top
        for g in range(g0 + 1, 8):
            part = parts[g]
            columns = [one_column(part, g0 * 8 + j) for j in range(8)]
            for j in range(8):
                factor = columns[j] * inverse[j]
                for k in range(j + 1, 8):
                    columns[k] = columns[k] - factor * ahead[j][k - j - 1]
                part = part - factor * lines[j]
            parts[g] = part
    return jnp.concatenate([(parts[g] * lax.rsqrt(pivots[g]))[:, K:] for g in range(8)], axis=0)


def matrix_kernel(grams, mat):
    both = grams[0:K, :]
    factor = inverse_factor(both[:, 0:K])
    image = small_dot(factor, both[:, K : 2 * K], ((1,), (1,)))
    rayleigh = small_dot(image, factor, ((1,), (1,)))
    other = 0.5 * small_dot(rayleigh, factor, ((0,), (0,)))
    fh, fl = halves(factor)
    oh, ol = halves(other)
    mat[...] = jnp.concatenate(
        [jnp.concatenate([fh, fh, oh, oh], axis=1), jnp.concatenate([fl, fl, ol, ol], axis=1)], axis=0
    )


def off_kernel(w0, w1, w2, w3, img_ref, out):
    acc = jnp.zeros((2 * K, 2 * K), F32)
    for c in range(3):
        for pair in (0, 2):
            left, right = [], []
            for r in (pair, pair + 1):
                left.append(jnp.concatenate(halves(slab((w0, w1, w2, w3)[r], c * 4)), axis=0))
                right.append(jnp.concatenate(halves(slab(img_ref, r * 3 + c)), axis=0))
            acc += lax.dot_general(
                jnp.concatenate(left, axis=1),
                jnp.concatenate(right, axis=1),
                (((1,), (1,)), ((), ())),
                preferred_element_type=F32,
            )
    half = acc[0:K, :] + acc[K : 2 * K, :]
    out[:, 0:K] = half[:, 0:K] + half[:, K : 2 * K]
    before = pltpu.roll(img_ref[pl.ds(FROWS, K), :], K, 1)
    out[:, K : 2 * K] = before[:, K : 2 * K]


def out_kernel(scal, both, r0, r1, r2, r3, out_hbm, diag_ref, off_ref, hold, cast, sem):
    back = (4 - scal[1]) & 3
    refs = (r0, r3, r2, r1)
    gram = both[0:K, :]
    raw = both[K : 2 * K, :]
    row = lax.broadcasted_iota(jnp.int32, (K, K), 0)
    column = lax.broadcasted_iota(jnp.int32, (K, K), 1)
    before = jnp.where(scal[3] == 0, (row == column).astype(F32), raw[:, K : 2 * K])
    factor = inverse_factor(gram[:, 0:K])
    fh, fl = halves(factor)
    matrix = jnp.concatenate([jnp.concatenate([fh, fh], axis=1), jnp.concatenate([fl, fl], axis=1)], axis=0)
    whole = K * NX

    def body(t, carry):
        c, big = t >> 2, t & 3
        values = swap_blocks(turn([slab(r, t) for r in refs], back))
        for xx in range(4):
            mix = lax.dot_general(
                matrix, jnp.concatenate(halves(values[xx]), axis=0), (((1,), (0,)), ((), ())), preferred_element_type=F32
            )
            hold[pl.ds(c * whole + big * 4 + xx, K, stride=NX), :] = mix[0:K, :] + mix[K : 2 * K, :]
        return carry

    def to_bf16(i, carry):
        at = pl.ds(pl.multiple_of(i * 128, 128), 128)
        cast[at, :] = hold[at, :].astype(BF16)
        return carry

    def copy(c):
        at = pl.ds(c * whole, whole)
        return pltpu.make_async_copy(cast.at[at, :], out_hbm.at[at, :], sem.at[c])

    for c in range(3):
        lax.fori_loop(4 * c, 4 * c + 4, body, 0)
        lax.fori_loop(c * (whole // 128), (c + 1) * (whole // 128), to_bf16, 0)
        copy(c).start()
    other = inverse_factor(before)
    image = small_dot(factor, gram[:, K : 2 * K], ((1,), (1,)))
    diag_ref[...] = small_dot(image, factor, ((1,), (1,)))
    off_ref[...] = small_dot(small_dot(factor, raw[:, 0:K]), other, ((1,), (1,)))
    for c in range(3):
        copy(c).wait()


def call(kernel, n_in, shapes, scratch=(), first=VM, rest=VM, params=PARAMS):
    return pl.pallas_call(
        kernel,
        out_shape=shapes,
        in_specs=[first] + [rest] * (n_in - 1),
        out_specs=jax.tree.map(lambda _: VM, shapes),
        scratch_shapes=list(scratch),
        compiler_params=params,
    )


def shift_x(value, d):
    return lax.ppermute(value, "dom", [(i, (i & 12) + ((i + d) & 3)) for i in range(16)])


def shift_y(value, d):
    return lax.ppermute(value, "dom", [(i, (i + 4 * d) & 15) for i in range(16)])


def halo_y(y_up, y_dn):
    h_dn = lax.ppermute(y_up, "dom", [(i, i + 4) for i in range(12)])
    h_up = lax.ppermute(y_dn, "dom", [(i + 4, i) for i in range(12)])
    return h_up, h_dn


def total(value, shift):
    parts = {}
    for d in (1, 3, 2):
        parts[d] = shift(value, d)
    return (value + parts[2]) + (parts[1] + parts[3])


def to_rows(packed):
    got = [packed[0]]
    for d in (1, 2, 3):
        got.append(shift_x(packed[d], d))
    return got


def exchange(near, images):
    own = total(near[0:K], shift_y)
    h_up, h_dn = halo_y(images[3], images[0])
    near = jnp.concatenate([own, near[K:]], axis=0)
    h_before = shift_x(near, 1)
    h_after = shift_x(near, 3)
    far = shift_x(own, 2)
    grams = (own + far) + (h_before[0:K] + h_after[0:K])
    return grams, (h_up, h_dn, h_before, h_after)


def blocks(start_vectors, face_x, face_y, face_z, masses, active):
    row = lax.axis_index("dom").astype(jnp.int32)
    scal = jnp.stack([active[0], row & 3, row, lax.axis_index("sub").astype(jnp.int32)]).astype(jnp.int32)
    start = start_vectors.reshape(3 * K * NX, LANES)
    fields = [f.reshape(NX, LANES) for f in (face_x, face_y, face_z, masses)]
    msg = f32(YROWS, LANES)
    zmsg = f32(ZROWS, LANES)
    near = f32(K + ZROWS, LANES)
    plane = pltpu.VMEM((NX, LANES), F32)
    columns = pltpu.VMEM((ZROWS, LANES), F32)
    wide = pltpu.CompilerParams(vmem_limit_bytes=67_000_000)
    hbm = pl.BlockSpec(memory_space=pl.ANY)
    msg_a, msg_b = f32(AROWS + NX, LANES), f32(BROWS, LANES)
    packed = call(
        pack_a_kernel,
        6,
        (msg_a,) * 4,
        (pltpu.VMEM((K * NX, LANES), F32),)
        + (plane,) * 4
        + (pltpu.SemaphoreType.DMA((1,)), pltpu.SemaphoreType.DMA((4,))),
        first=SM,
        rest=hbm,
        params=wide,
    )(scal, start, *fields)
    got_a = to_rows(packed)
    packed = call(
        pack_b_kernel,
        2,
        (msg_b,) * 4,
        (pltpu.VMEM((2 * K * NX, LANES), F32), pltpu.SemaphoreType.DMA((2,))),
        first=SM,
        rest=hbm,
        params=wide,
    )(scal, start)
    got_b = to_rows(packed)
    *early, z_a = call(unpack_a_kernel, 5, (msg_a,) * 4 + (f32(K + NX, LANES),), first=SM)(scal, *got_a)
    hv_a = halo_y(early[3], early[0])
    *v, edge_dn, edge_up, z_edge = call(
        unpack_b_kernel, 10, (msg,) * 4 + (msg_b, msg_b, zmsg), first=SM
    )(scal, *got_b, *early, z_a)
    hv_b = halo_y(edge_up, edge_dn)
    h_before, h_after = shift_x(z_edge, 1), shift_x(z_edge, 3)
    acc = pltpu.VMEM((4 * K, 2 * K), F32)
    *av, fld, near_new, hv_z, h_up, h_dn = call(
        first_kernel, 11, (msg,) * 4 + (f32(10 * NX, LANES), near, zmsg, msg, msg), (acc,), first=SM
    )(scal, *v, *hv_a, *hv_b, h_before, h_after)
    hv = (h_up, h_dn)
    mat_shape = jax.ShapeDtypeStruct((2 * K, 4 * K), BF16)
    grams, ha = exchange(near_new, av)
    mat = call(matrix_kernel, 1, mat_shape)(grams)
    out = call(
        functools.partial(step_kernel, False),
        18,
        (msg,) * 8 + (near, msg, msg, zmsg, f32(24, LANES)),
        (acc, columns),
        first=SM,
    )(scal, *v, *av, fld, mat, *hv, hv_z, *ha)
    v, av, (near_new, n_up, n_dn, n_z, rows) = out[:4], out[4:8], out[8:]
    grams, ha = exchange(near_new, av)
    mat = call(matrix_kernel, 1, mat_shape)(grams)
    side = pltpu.VMEM((YROWS, LANES), F32)
    part = f32(FROWS, LANES)
    img, grams, *packed = call(
        functools.partial(step_kernel, True),
        19,
        (f32(FROWS + K, LANES), f32(K, LANES)) + (part,) * 4,
        (acc, columns, side, side, columns) + (side,) * 8,
        first=SM,
    )(scal, *v, *av, fld, mat, n_up, n_dn, n_z, *ha, rows)
    behind = [(i, i + 1) for i in range(15)]
    before = lax.ppermute(img, "sub", behind)
    got = to_rows(packed)
    raw_off = call(off_kernel, 5, f32(K, 2 * K))(*packed, before)
    both = jnp.concatenate([grams, raw_off], axis=0)
    both = total(total(both, shift_y), shift_x)
    hbm = pl.BlockSpec(memory_space=pl.ANY)
    out, diag, off = pl.pallas_call(
        out_kernel,
        out_shape=(jax.ShapeDtypeStruct((3 * K * NX, LANES), BF16), f32(K, K), f32(K, K)),
        in_specs=[SM] + [VM] * 5,
        out_specs=(hbm, VM, VM),
        scratch_shapes=[
            pltpu.VMEM((3 * K * NX, LANES), F32),
            pltpu.VMEM((3 * K * NX, LANES), BF16),
            pltpu.SemaphoreType.DMA((3,)),
        ],
        compiler_params=PARAMS,
        name="rows",
    )(scal, both, *got)
    return (out.reshape(1, 3, K, 1, NX, LANES), diag[None], off[None])


def solution(mesh):
    placed = (
        P("sub", None, None, "dom", None, None),
        P("sub", "dom", None, None),
        P("sub", "dom", None, None),
        P("sub", "dom", None, None),
        P("sub", "dom", None, None),
        P("sub"),
    )
    return jax.shard_map(
        blocks,
        mesh=mesh,
        in_specs=placed,
        out_specs=(
            P("sub", None, None, "dom", None, None),
            P("sub", None, None),
            P("sub", None, None),
        ),
        check_vma=False,
    )
```
